128 devices in a mesh: seq: 8 (over z, y_hi), dp: 16 (over y_lo, x, core).
Axes of the slice: x: 4, y: 4 (y_hi: 2, y_lo: 2; y = y_hi * 2 + y_lo), z: 4, core: 2. Of those that a mesh axis runs over, the one named last changes fastest.
Arguments:
- queries: bfloat16 [16, 2048, 1024], P('dp', 'seq'), may hold values from -24 to 24
- keys: bfloat16 [16, 2048, 1024], P('dp', 'seq'), may hold values from -4 to 4
- values: bfloat16 [16, 2048, 1024], P('dp', 'seq'), may hold values from -6 to 6
- out_proj: bfloat16 [1024, 2048], P('dp'), may hold values from -0.1875 to 0.1875
- grad_out: bfloat16 [16, 2048, 2048], P('dp', 'seq'), may hold values from -24 to 24
Outputs:
- grad_qkv: bfloat16 [16, 2048, 3072], P('dp', 'seq')
- grad_weight: float32 [1024, 2048], P('dp')
The draws below stay inside these ranges and needn't reach their ends.
All inputs are finite; a program needn't handle non-finite values.
Results may differ from the reference program's by a relative error of at most 0.0058.
Values may be sent and summed in bfloat16 or wider, within the bound.
A program may use at most 64 MiB of HBM per device.

```python
import jax
import jax.numpy as jnp
from jax import lax

D = 2048
HEADS = 16
HEAD_DIM = 64
SEQ_LEN = 2048
BATCH = 16


def qk_pair(key):
    base = jax.random.fold_in(key, 11)
    key_q, key_k = jax.random.split(base, 2)
    shape = (BATCH, SEQ_LEN, HEADS, HEAD_DIM)
    query_part = jnp.clip(jax.random.normal(key_q, shape), -4.0, 4.0)
    key_part = jnp.clip(jax.random.normal(key_k, shape), -4.0, 4.0)
    flat = (BATCH, SEQ_LEN, HEADS * HEAD_DIM)
    return (query_part.reshape(flat), key_part.reshape(flat))


def draw_queries(key, part):
    return qk_pair(key)[0].astype(jnp.bfloat16)


def draw_keys(key, part):
    return qk_pair(key)[1].astype(jnp.bfloat16)


def levels(rng, dims, pieces, smallest, top_value):
    def one(axis_at, shards_of):
        steps = jax.random.uniform(jax.random.fold_in(jax.random.fold_in(rng, 6), axis_at), (shards_of,), jnp.float32, smallest / len(pieces), top_value / len(pieces))
        return jnp.repeat(jnp.exp(steps), dims[axis_at] // shards_of).reshape((-1,) + (1,) * (len(dims) - axis_at - 1))

    loudness = one(*pieces[0])
    for cut in pieces[1:]:
        loudness = loudness * one(*cut)
    return loudness


def centred(rng, shape, width, most, cuts=(), dtype=jnp.bfloat16):
    values = width * jax.random.normal(rng, shape, jnp.float32)
    if cuts:
        values = values * levels(rng, shape, cuts, -0.22, 0.18)
    return jnp.clip(values, -most, most).astype(dtype)


def setup_inputs(seed: int = 0) -> dict:
    splits = jax.random.split(jax.random.key(seed), 6)
    queries = draw_queries(jax.random.fold_in(splits[5], 71), 0)
    keys = draw_keys(jax.random.fold_in(splits[5], 71), 0)
    values = centred(splits[2], (BATCH, SEQ_LEN, HEADS * HEAD_DIM), 1.0, 6.0, ((0, 16), (1, 8)))
    out_proj = centred(splits[3], (HEADS * HEAD_DIM, D), (HEADS * HEAD_DIM) ** -0.5, 0.1875, ((0, 16),))
    grad_out = centred(splits[4], (BATCH, SEQ_LEN, D), 4.0, 24.0, ((0, 16), (1, 8)))
    return {"queries": queries, "keys": keys, "values": values, "out_proj": out_proj, "grad_out": grad_out}


def head_terms(packed):
    q_head, k_head, v_head, g_head = packed
    scaling = HEAD_DIM ** -0.5
    scores = jnp.dot(q_head, k_head.T, preferred_element_type=jnp.float32) * scaling
    row_max = jnp.max(scores, axis=1, keepdims=True)
    exp_scores = jnp.exp(scores - row_max)
    probs = exp_scores / jnp.sum(exp_scores, axis=1, keepdims=True)
    probs_low = probs.astype(jnp.bfloat16)
    attn_out = jnp.dot(probs_low, v_head, preferred_element_type=jnp.float32).astype(jnp.bfloat16)
    grad_prob = jnp.dot(g_head, v_head.T, preferred_element_type=jnp.float32)
    row_dot = jnp.sum(probs * grad_prob, axis=1, keepdims=True)
    grad_score = (scaling * probs * (grad_prob - row_dot)).astype(jnp.bfloat16)
    grad_q = jnp.dot(grad_score, k_head, preferred_element_type=jnp.float32).astype(jnp.bfloat16)
    grad_k = jnp.dot(grad_score.T, q_head, preferred_element_type=jnp.float32).astype(jnp.bfloat16)
    grad_v = jnp.dot(probs_low.T, g_head, preferred_element_type=jnp.float32).astype(jnp.bfloat16)
    return attn_out, grad_q, grad_k, grad_v


def split_heads(array):
    return array.reshape(BATCH, SEQ_LEN, HEADS, HEAD_DIM).transpose(0, 2, 1, 3).reshape(BATCH * HEADS, SEQ_LEN, HEAD_DIM)


def merge_heads(array):
    return array.reshape(BATCH, HEADS, SEQ_LEN, HEAD_DIM).transpose(0, 2, 1, 3).reshape(BATCH, SEQ_LEN, HEADS * HEAD_DIM)


def reference(queries, keys, values, out_proj, grad_out):
    flat_grad = grad_out.reshape(BATCH * SEQ_LEN, D)
    grad_attn = jnp.dot(flat_grad, out_proj.T, preferred_element_type=jnp.float32).astype(jnp.bfloat16)
    grad_attn = grad_attn.reshape(BATCH, SEQ_LEN, HEADS * HEAD_DIM)
    results = lax.map(head_terms, (split_heads(queries), split_heads(keys), split_heads(values), split_heads(grad_attn)))
    attn_out = merge_heads(results[0])
    grad_qkv = jnp.concatenate([merge_heads(results[1]), merge_heads(results[2]), merge_heads(results[3])], axis=2)
    grad_weight = jnp.dot(attn_out.reshape(BATCH * SEQ_LEN, HEADS * HEAD_DIM).T, flat_grad, preferred_element_type=jnp.float32)
    return grad_qkv, grad_weight
```

```python
import math

import jax
import jax.numpy as jnp
from jax import lax
from jax.experimental import pallas as pl
from jax.experimental.pallas import tpu as pltpu
from jax.sharding import PartitionSpec as P

HEAD_DIM = 64

ROWS = 256
CHUNK = 512
LANES = 128
EXP_SCALE = HEAD_DIM ** (-0.5) * math.log2(math.e)
F32 = jnp.float32
BF16 = jnp.bfloat16


def split_heads(columns):
    row = lax.broadcasted_iota(jnp.int32, columns.shape, 0)
    zeros = jnp.zeros_like(columns)
    return jnp.concatenate(
        [jnp.where(row < HEAD_DIM, columns, zeros), jnp.where(row < HEAD_DIM, zeros, columns)], axis=1
    )


def merge_heads(wide):
    first, second = wide[:, :ROWS], wide[:, ROWS:]
    row = lax.broadcasted_iota(jnp.int32, first.shape, 0)
    return jnp.where(row < HEAD_DIM, first, second)


def dot(a, b):
    return jnp.dot(a, b, preferred_element_type=F32)


def attention_kernel(
    q_ref, k_ref, v_ref, g_ref, out_ref, dq_ref, dk_ref, dv_ref,
    k_t, v_t, score, prob, q_t, out_t, inv_sum, out_all, g_t, q_l, g_l, dq_t, dk_sum, dv_sum,
):
    blocks = q_ref.shape[0]
    length = blocks * ROWS
    chunks = length // CHUNK
    wide = 2 * ROWS
    k_rows = k_ref.reshape(length, LANES)
    v_rows = v_ref.reshape(length, LANES)
    for i in range(blocks):
        k_t[:, i * ROWS : (i + 1) * ROWS] = k_ref[i].astype(F32).T.astype(BF16)
        v_t[:, i * ROWS : (i + 1) * ROWS] = v_ref[i].astype(F32).T.astype(BF16)
    dk_sum[...] = jnp.zeros_like(dk_sum)
    dv_sum[...] = jnp.zeros_like(dv_sum)

    def forward(i, carry):
        q_t[...] = split_heads(q_ref[i].astype(F32).T).astype(BF16)

        def score_chunk(c, top):
            keys = pl.ds(pl.multiple_of(c * CHUNK, CHUNK), CHUNK)
            s = dot(k_rows[keys, :], q_t[...])
            score[keys, :] = s
            return jnp.maximum(top, jnp.max(s.reshape(CHUNK // 8, 8, wide), axis=0))

        top = lax.fori_loop(0, chunks, score_chunk, jnp.full((8, wide), -jnp.inf, F32), unroll=True)
        top = jnp.max(top, axis=0, keepdims=True)
        out_t[...] = jnp.zeros_like(out_t)

        def prob_chunk(c, total):
            keys = pl.ds(pl.multiple_of(c * CHUNK, CHUNK), CHUNK)
            p = jnp.exp2((score[keys, :] - top) * EXP_SCALE)
            low = p.astype(BF16)
            prob[i, keys, :] = low
            out_t[...] += dot(v_t[:, keys], low)
            return total + jnp.sum(p.reshape(CHUNK // 8, 8, wide), axis=0)

        total = lax.fori_loop(0, chunks, prob_chunk, jnp.zeros((8, wide), F32), unroll=True)
        inverse = 1.0 / jnp.sum(total, axis=0, keepdims=True)
        inv_sum[i] = jnp.broadcast_to(inverse, (8, wide))
        merged = merge_heads(out_t[...] * inverse)
        out_all[i] = merged
        out_ref[i] = merged.T.astype(BF16)
        return carry

    lax.fori_loop(0, blocks, forward, 0)

    def backward(i, carry):
        inverse = inv_sum[i, 0:1, :]
        g = g_ref[i].astype(F32).T
        g_split = split_heads(g)
        g_t[...] = g_split.astype(BF16)
        g_l[...] = (g_split * inverse).T.astype(BF16)
        q_l[...] = (split_heads(q_ref[i].astype(F32).T) * (inverse * HEAD_DIM ** (-0.5))).T.astype(BF16)
        product = out_all[i] * g
        row_dot = jnp.concatenate(
            [
                jnp.sum(product[:HEAD_DIM], axis=0, keepdims=True),
                jnp.sum(product[HEAD_DIM:], axis=0, keepdims=True),
            ],
            axis=1,
        )
        dq_t[...] = jnp.zeros_like(dq_t)

        def grad_chunk(c, carry):
            keys = pl.ds(pl.multiple_of(c * CHUNK, CHUNK), CHUNK)
            grad_prob = dot(v_rows[keys, :], g_t[...])
            low = prob[i, keys, :]
            grad_score = (low.astype(F32) * (grad_prob - row_dot)).astype(BF16)
            dv_sum[keys, :] += dot(low, g_l[...])
            dk_sum[keys, :] += dot(grad_score, q_l[...])
            dq_t[...] += dot(k_t[:, keys], grad_score)
            return carry

        lax.fori_loop(0, chunks, grad_chunk, 0, unroll=True)
        dq_ref[i] = merge_heads(dq_t[...] * (inverse * HEAD_DIM ** (-0.5))).T.astype(BF16)
        return carry

    lax.fori_loop(0, blocks, backward, 0)
    dk_ref[...] = dk_sum[...].astype(BF16).reshape(dk_ref.shape)
    dv_ref[...] = dv_sum[...].astype(BF16).reshape(dv_ref.shape)


def attention(q, k, v, g):
    length, columns = q.shape
    blocks = length // ROWS
    shape = (blocks, ROWS, columns)
    vmem = pltpu.VMEM
    results = pl.pallas_call(
        attention_kernel,
        out_shape=[jax.ShapeDtypeStruct(shape, BF16)] * 4,
        in_specs=[pl.BlockSpec(memory_space=vmem)] * 4,
        out_specs=[pl.BlockSpec(memory_space=vmem)] * 4,
        scratch_shapes=[
            vmem((LANES, length), BF16),
            vmem((LANES, length), BF16),
            vmem((length, 2 * ROWS), F32),
            vmem((blocks, length, 2 * ROWS), BF16),
            vmem((LANES, 2 * ROWS), BF16),
            vmem((LANES, 2 * ROWS), F32),
            vmem((blocks, 8, 2 * ROWS), F32),
            vmem((blocks, LANES, ROWS), F32),
            vmem((LANES, 2 * ROWS), BF16),
            vmem((2 * ROWS, LANES), BF16),
            vmem((2 * ROWS, LANES), BF16),
            vmem((LANES, 2 * ROWS), F32),
            vmem((length, LANES), F32),
            vmem((length, LANES), F32),
        ],
        compiler_params=pltpu.CompilerParams(vmem_limit_bytes=48 << 20),
    )(*(x.reshape(shape) for x in (q, k, v, g)))
    return [x.reshape(length, columns) for x in results]


def on_device(queries, keys, values, out_proj, grad_out):
    grad_tokens = grad_out[0]
    grad_attn = lax.dot_general(
        grad_tokens,
        lax.all_gather(out_proj, "dp", axis=0, tiled=True),
        (((1,), (1,)), ((), ())),
        preferred_element_type=jnp.float32,
    ).astype(jnp.bfloat16)
    head_q, head_k, head_v, head_g = (
        lax.all_to_all(queries[0], "seq", split_axis=1, concat_axis=0, tiled=True),
        lax.all_to_all(keys[0], "seq", split_axis=1, concat_axis=0, tiled=True),
        lax.all_to_all(values[0], "seq", split_axis=1, concat_axis=0, tiled=True),
        lax.all_to_all(grad_attn, "seq", split_axis=1, concat_axis=0, tiled=True),
    )
    head_out, head_dq, head_dk, head_dv = attention(head_q, head_k, head_v, head_g)
    token_out, token_dq, token_dk, token_dv = (
        lax.all_to_all(head_out, "seq", split_axis=0, concat_axis=1, tiled=True),
        lax.all_to_all(head_dq, "seq", split_axis=0, concat_axis=1, tiled=True),
        lax.all_to_all(head_dk, "seq", split_axis=0, concat_axis=1, tiled=True),
        lax.all_to_all(head_dv, "seq", split_axis=0, concat_axis=1, tiled=True),
    )
    grad_qkv = jnp.concatenate([token_dq, token_dk, token_dv], axis=1)[None]
    share = lax.psum_scatter(
        lax.dot_general(
            token_out, grad_tokens, (((0,), (0,)), ((), ())), preferred_element_type=jnp.float32
        ),
        "dp",
        scatter_dimension=0,
        tiled=True,
    )
    grad_weight = lax.psum(share, "seq")
    return (grad_qkv, grad_weight)


def solution(mesh):
    return jax.shard_map(
        on_device,
        mesh=mesh,
        in_specs=(
            P("dp", "seq", None),
            P("dp", "seq", None),
            P("dp", "seq", None),
            P("dp", None),
            P("dp", "seq", None),
        ),
        out_specs=(P("dp", "seq", None), P("dp", None)),
        check_vma=False,
    )
```

```python
import functools
import math

import jax
import jax.numpy as jnp
from jax import lax
from jax.experimental import pallas as pl
from jax.experimental.pallas import tpu as pltpu
from jax.sharding import PartitionSpec as P

HEAD_DIM = 64
LANES = 2 * HEAD_DIM
CHUNK = 512
SCALING = HEAD_DIM ** (-0.5)
EXP_SCALE = SCALING * math.log2(math.e)
F32 = jnp.float32
BF16 = jnp.bfloat16


def dot(a, b):
    return jnp.dot(a, b, preferred_element_type=F32)


def dot_nt(a, b):
    return lax.dot_general(a, b, (((1,), (1,)), ((), ())), preferred_element_type=F32)


def split_heads(columns):
    row = lax.broadcasted_iota(jnp.int32, columns.shape, 0)
    zeros = jnp.zeros_like(columns)
    return jnp.concatenate(
        [jnp.where(row < HEAD_DIM, columns, zeros), jnp.where(row < HEAD_DIM, zeros, columns)], axis=1
    )


def merge_heads(wide):
    rows = wide.shape[1] // 2
    first, second = wide[:, :rows], wide[:, rows:]
    row = lax.broadcasted_iota(jnp.int32, first.shape, 0)
    return jnp.where(row < HEAD_DIM, first, second)


def kernel(
    n, rows, width,
    q_ref, k_ref, v_ref, w_ref, go_ref, dqkv_ref, gw_ref,
    q_in, k_in, v_in, g_in, w_all, go, k_t, v_t,
    score, prob, q_t, out_t, inv_sum, out_all, g_t, q_l, g_l, dq_t, dk_sum, dv_sum,
    g_out, o_out, o_in, o_rows, own_part, sib_out, sib_in, rs_out, rs_in,
    total, total_low, gs_in, done, dq_out, dk_out, dv_out,
    qkv_send, qkv_recv, w_send, w_recv, ws_send, ws_recv, g_send, g_recv, o_send, o_recv,
    sib_send, sib_recv, rs_send, rs_recv, gs_send, gs_recv, gw_send, gw_recv,
    d_send, d_recv, local_sem,
):
    s = lax.axis_index("seq")
    d = lax.axis_index("dp")
    chip, core = d // 2, lax.rem(d, 2)
    length = n * rows
    chunks = length // CHUNK
    wide = 2 * rows
    half = HEAD_DIM
    columns = width // n

    def ahead(base, i):
        return lax.rem(base + i, n)

    def behind(base, i):
        return lax.rem(base + n - i, n)

    def block(index, size):
        return pl.ds(pl.multiple_of(index * size, size), size)

    def remote(src, dst, send, recv, where):
        return pltpu.make_async_remote_copy(
            src_ref=src, dst_ref=dst, send_sem=send, recv_sem=recv,
            device_id=where, device_id_type=pl.DeviceIdType.MESH,
        )

    my_half = block(core, half)
    sibling = {"dp": 2 * chip + 1 - core}

    def qkv_copy(t, i):
        src, dst = ((k_ref, k_in), (v_ref, v_in), (q_ref, q_in))[t]
        peer = ahead(s, i)
        return remote(
            src.at[0, :, block(peer, LANES)], dst.at[i], qkv_send.at[t, i], qkv_recv.at[t, i], {"seq": peer}
        )

    def w_copy(j):
        return remote(
            w_ref, w_all.at[j, my_half, :], w_send.at[j], w_recv.at[j], {"dp": 2 * ahead(chip, j) + core}
        )

    def ws_first():
        return remote(w_ref, w_all.at[0, my_half, :], ws_send.at[0], ws_recv.at[0], sibling)

    def ws_copy(j):
        part = w_all.at[j, my_half, :]
        return remote(part, part, ws_send.at[j], ws_recv.at[j], sibling)

    def g_copy(i):
        return remote(g_out.at[i], g_in.at[i], g_send.at[i], g_recv.at[i], {"seq": ahead(s, i)})

    def o_copy(i):
        return remote(o_out.at[i], o_in.at[i], o_send.at[i], o_recv.at[i], {"seq": behind(s, i)})

    def sib_copy():
        return remote(sib_out, sib_in, sib_send.at[0], sib_recv.at[0], sibling)

    def rs_copy(j):
        return remote(
            rs_out.at[j], rs_in.at[j], rs_send.at[j], rs_recv.at[j], {"dp": 2 * ahead(chip, j) + core}
        )

    def gs_copy(i):
        peer = ahead(s, i)
        return remote(total_low.at[peer], gs_in.at[i], gs_send.at[i], gs_recv.at[i], {"seq": peer})

    def gw_copy(i):
        return remote(
            done, gw_ref.at[:, block(s, columns)], gw_send.at[i], gw_recv.at[i], {"seq": ahead(s, i)}
        )

    def d_copy(t, i):
        src = (dq_out, dk_out, dv_out)[t]
        dst = dqkv_ref.at[0, :, block(t * n + s, LANES)]
        return remote(src.at[i], dst, d_send.at[t, i], d_recv.at[t, i], {"seq": behind(s, i)})

    def each(first, step):
        def body(i, carry):
            step(i)
            return carry

        lax.fori_loop(first, n, body, 0)

    local = [
        pltpu.make_async_copy(k_ref.at[0, :, block(s, LANES)], k_in.at[0], local_sem.at[0]),
        pltpu.make_async_copy(v_ref.at[0, :, block(s, LANES)], v_in.at[0], local_sem.at[1]),
        pltpu.make_async_copy(q_ref.at[0, :, block(s, LANES)], q_in.at[0], local_sem.at[2]),
        pltpu.make_async_copy(w_ref, w_all.at[0, my_half, :], local_sem.at[3]),
        pltpu.make_async_copy(go_ref.at[0], go, local_sem.at[4]),
    ]
    for copy in local:
        copy.start()

    barrier = pltpu.get_barrier_semaphore()

    def greet(i):
        pl.semaphore_signal(
            barrier, inc=1, device_id={"seq": ahead(s, i)}, device_id_type=pl.DeviceIdType.MESH
        )
        pl.semaphore_signal(
            barrier, inc=1, device_id={"dp": 2 * ahead(chip, i) + core}, device_id_type=pl.DeviceIdType.MESH
        )

    each(1, greet)
    pl.semaphore_signal(barrier, inc=1, device_id=sibling, device_id_type=pl.DeviceIdType.MESH)
    pl.semaphore_wait(barrier, 2 * (n - 1) + 1)

    def send_first(i):
        qkv_copy(0, i).start()
        w_copy(i).start()

    ws_first().start()
    each(1, send_first)
    each(1, lambda i: qkv_copy(1, i).start())
    each(1, lambda i: qkv_copy(2, i).start())
    for copy in local:
        copy.wait()

    dk_sum[...] = jnp.zeros_like(dk_sum)
    dv_sum[...] = jnp.zeros_like(dv_sum)

    def turn(src, dst, i):
        dst[:, block(i, rows)] = src[i].astype(F32).T.astype(BF16)

    turn(k_in, k_t, 0)
    turn(v_in, v_t, 0)

    def arrive(i):
        qkv_copy(0, i).wait_recv()
        turn(k_in, k_t, i)
        qkv_copy(1, i).wait_recv()
        turn(v_in, v_t, i)

    each(1, arrive)

    k_rows = k_in.reshape(length, LANES)
    v_rows = v_in.reshape(length, LANES)

    def grad_attn(j):
        peer = behind(chip, j)
        i = behind(peer, s)
        g = dot_nt(go[...], w_all[j]).astype(BF16)

        @pl.when(i == 0)
        def _():
            g_in[0] = g

        @pl.when(i > 0)
        def _():
            g_out[i] = g
            g_copy(i).start()

    def forward(i, carry):
        @pl.when(i > 0)
        def _():
            qkv_copy(2, i).wait_recv()

        q_t[...] = split_heads(q_in[i].astype(F32).T).astype(BF16)

        def score_chunk(c, top):
            keys = block(c, CHUNK)
            x = dot(k_rows[keys, :], q_t[...])
            score[keys, :] = x
            return jnp.maximum(top, jnp.max(x.reshape(CHUNK // 8, 8, wide), axis=0))

        top = lax.fori_loop(0, chunks, score_chunk, jnp.full((8, wide), -jnp.inf, F32), unroll=True)
        top = jnp.max(top, axis=0, keepdims=True)
        out_t[...] = jnp.zeros_like(out_t)

        def prob_chunk(c, norm):
            keys = block(c, CHUNK)
            p = jnp.exp2((score[keys, :] - top) * EXP_SCALE)
            low = p.astype(BF16)
            prob[i, keys, :] = low
            out_t[...] += dot(v_t[:, keys], low)
            return norm + jnp.sum(p.reshape(CHUNK // 8, 8, wide), axis=0)

        norm = lax.fori_loop(0, chunks, prob_chunk, jnp.zeros((8, wide), F32), unroll=True)
        inverse = 1.0 / jnp.sum(norm, axis=0, keepdims=True)
        inv_sum[i] = jnp.broadcast_to(inverse, (8, wide))
        merged = merge_heads(out_t[...] * inverse)
        out_all[i] = merged

        @pl.when(i == 0)
        def _():
            o_in[0] = merged.astype(BF16)

        @pl.when(i > 0)
        def _():
            o_out[i] = merged.astype(BF16)
            o_copy(i).start()
            w_copy(i).wait_recv()
            ws_copy(i).start()
            ws_copy(i - 1).wait_recv()
            grad_attn(i - 1)

        return carry

    lax.fori_loop(0, n, forward, 0)
    ws_copy(n - 1).wait_recv()
    grad_attn(n - 1)

    def weight_part():
        each(1, lambda i: o_copy(i).wait_recv())
        for i in range(n):
            o_rows[i * half : (i + 1) * half, :] = o_in[i, my_half, :]
            o_rows[(n + i) * half : (n + i + 1) * half, :] = o_in[i, block(1 - core, half), :]
        for c in range(n):
            cut = slice(c * columns, (c + 1) * columns)
            part = dot(o_rows[...], go[:, cut])
            own_part[:, :, cut] = part[: n * half].reshape(n, half, columns).astype(BF16)
            sib_out[:, :, cut] = part[n * half :].reshape(n, half, columns).astype(BF16)
        sib_copy().start()

    def pair_sum(j):
        i = behind(ahead(chip, j), s)
        return own_part[i].astype(F32) + sib_in[i].astype(F32)

    def share():
        sib_copy().wait_recv()

        def send(j):
            rs_out[j] = pair_sum(j).astype(BF16)
            rs_copy(j).start()

        each(1, send)

    def backward(i, carry):
        @pl.when(i > 0)
        def _():
            g_copy(i).wait_recv()

        inverse = inv_sum[i, 0:1, :]
        g = g_in[i].astype(F32).T
        g_split = split_heads(g)
        g_t[...] = g_split.astype(BF16)
        g_l[...] = (g_split * inverse).T.astype(BF16)
        q_l[...] = (split_heads(q_in[i].astype(F32).T) * (inverse * SCALING)).T.astype(BF16)
        product = out_all[i] * g
        row_dot = jnp.concatenate(
            [
                jnp.sum(product[:half], axis=0, keepdims=True),
                jnp.sum(product[half:], axis=0, keepdims=True),
            ],
            axis=1,
        )
        dq_t[...] = jnp.zeros_like(dq_t)

        def grad_chunk(c, carry):
            keys = block(c, CHUNK)
            grad_prob = dot(v_rows[keys, :], g_t[...])
            low = prob[i, keys, :]
            grad_score = (low.astype(F32) * (grad_prob - row_dot)).astype(BF16)
            dv_sum[keys, :] += dot(low, g_l[...])
            dk_sum[keys, :] += dot(grad_score, q_l[...])
            dq_t[...] += dot(k_t[:, keys], grad_score)
            return carry

        lax.fori_loop(0, chunks, grad_chunk, 0, unroll=True)
        grad_q = merge_heads(dq_t[...] * (inverse * SCALING)).T.astype(BF16)

        @pl.when(i == 0)
        def _():
            dqkv_ref[0, :, block(s, LANES)] = grad_q
            weight_part()

        @pl.when(i > 0)
        def _():
            dq_out[i] = grad_q
            d_copy(0, i).start()

        @pl.when(i == 1)
        def _():
            share()

        return carry

    lax.fori_loop(0, n, backward, 0)

    dqkv_ref[0, :, block(n + s, LANES)] = dk_sum[0:rows, :].astype(BF16)
    dqkv_ref[0, :, block(2 * n + s, LANES)] = dv_sum[0:rows, :].astype(BF16)

    def finish(i):
        dk_out[i] = dk_sum[block(i, rows), :].astype(BF16)
        d_copy(1, i).start()
        dv_out[i] = dv_sum[block(i, rows), :].astype(BF16)
        d_copy(2, i).start()

    each(1, finish)

    each(1, lambda j: rs_copy(j).wait_recv())
    mine = behind(chip, s)
    for c in range(n):
        cut = slice(c * columns, (c + 1) * columns)
        x = own_part[mine, :, cut].astype(F32) + sib_in[mine, :, cut].astype(F32)
        for j in range(1, n):
            x += rs_in[j, :, cut].astype(F32)
        total[c] = x
        total_low[c] = x.astype(BF16)
    each(1, lambda i: gs_copy(i).start())
    each(1, lambda i: gs_copy(i).wait_recv())
    x = total[s]
    for i in range(1, n):
        x += gs_in[i].astype(F32)
    done[...] = x
    each(1, lambda i: gw_copy(i).start())
    gw_ref[:, block(s, columns)] = x

    def arrivals(i):
        gw_copy(i).wait_recv()
        for t in range(3):
            d_copy(t, i).wait_recv()

    each(1, arrivals)

    def sent(i):
        for t in range(3):
            qkv_copy(t, i).wait_send()
            d_copy(t, i).wait_send()
        w_copy(i).wait_send()
        ws_copy(i).wait_send()
        g_copy(i).wait_send()
        o_copy(i).wait_send()
        rs_copy(i).wait_send()
        gs_copy(i).wait_send()
        gw_copy(i).wait_send()

    ws_first().wait_send()
    sib_copy().wait_send()
    each(1, sent)


def on_device(n, queries, keys, values, out_proj, grad_out):
    rows, features = queries.shape[1:]
    share_rows, width = out_proj.shape
    length = n * rows
    wide = 2 * rows
    columns = width // n
    vmem = pltpu.VMEM
    dma = pltpu.SemaphoreType.DMA
    flat = vmem((n, rows, LANES), BF16)
    turned = vmem((n, LANES, rows), BF16)
    shares = vmem((n, HEAD_DIM, width), BF16)
    return pl.pallas_call(
        functools.partial(kernel, n, rows, width),
        out_shape=(
            jax.ShapeDtypeStruct((1, rows, 3 * features), BF16),
            jax.ShapeDtypeStruct((share_rows, width), F32),
        ),
        in_specs=[pl.BlockSpec(memory_space=pl.ANY)] * 5,
        out_specs=[pl.BlockSpec(memory_space=vmem)] * 2,
        scratch_shapes=[
            flat, flat, flat, flat,
            vmem((n, LANES, width), BF16),
            vmem((rows, width), BF16),
            vmem((LANES, length), BF16),
            vmem((LANES, length), BF16),
            vmem((length, wide), F32),
            vmem((n, length, wide), BF16),
            vmem((LANES, wide), BF16),
            vmem((LANES, wide), F32),
            vmem((n, 8, wide), F32),
            vmem((n, LANES, rows), F32),
            vmem((LANES, wide), BF16),
            vmem((wide, LANES), BF16),
            vmem((wide, LANES), BF16),
            vmem((LANES, wide), F32),
            vmem((length, LANES), F32),
            vmem((length, LANES), F32),
            flat, turned, turned,
            vmem((2 * n * HEAD_DIM, rows), BF16),
            shares, shares, shares, shares, shares,
            vmem((n, HEAD_DIM, columns), F32),
            vmem((n, HEAD_DIM, columns), BF16),
            vmem((n, HEAD_DIM, columns), BF16),
            vmem((HEAD_DIM, columns), F32),
            flat, flat, flat,
            dma((3, n)), dma((3, n)),
            dma((n,)), dma((n,)), dma((n,)), dma((n,)),
            dma((n,)), dma((n,)), dma((n,)), dma((n,)),
            dma((1,)), dma((1,)), dma((n,)), dma((n,)),
            dma((n,)), dma((n,)), dma((n,)), dma((n,)),
            dma((3, n)), dma((3, n)), dma((5,)),
        ],
        compiler_params=pltpu.CompilerParams(
            collective_id=0, has_side_effects=True, vmem_limit_bytes=60 << 20
        ),
    )(queries, keys, values, out_proj, grad_out)


def solution(mesh):
    return jax.shard_map(
        functools.partial(on_device, mesh.shape["seq"]),
        mesh=mesh,
        in_specs=(
            P("dp", "seq", None),
            P("dp", "seq", None),
            P("dp", "seq", None),
            P("dp", None),
            P("dp", "seq", None),
        ),
        out_specs=(P("dp", "seq", None), P("dp", None)),
        check_vma=False,
    )
```

```python
import functools
import math

import jax
import jax.numpy as jnp
from jax import lax
from jax.experimental import pallas as pl
from jax.experimental.pallas import tpu as pltpu
from jax.sharding import PartitionSpec as P

HEAD_DIM = 64
LANES = 2 * HEAD_DIM
X = 4
CHUNK = 512
SCALING = HEAD_DIM ** (-0.5)
EXP_SCALE = SCALING * math.log2(math.e)
F32 = jnp.float32
BF16 = jnp.bfloat16


def dot(a, b):
    return jnp.dot(a, b, preferred_element_type=F32)


def dot_nt(a, b):
    return lax.dot_general(a, b, (((1,), (1,)), ((), ())), preferred_element_type=F32)


def split_heads(columns):
    row = lax.broadcasted_iota(jnp.int32, columns.shape, 0)
    zeros = jnp.zeros_like(columns)
    return jnp.concatenate(
        [jnp.where(row < HEAD_DIM, columns, zeros), jnp.where(row < HEAD_DIM, zeros, columns)], axis=1
    )


def merge_heads(wide):
    rows = wide.shape[1] // 2
    first, second = wide[:, :rows], wide[:, rows:]
    row = lax.broadcasted_iota(jnp.int32, first.shape, 0)
    return jnp.where(row < HEAD_DIM, first, second)


def kernel(
    n, rows, width,
    q_ref, k_ref, v_ref, w_ref, go_ref, dqkv_ref, gw_ref,
    q_in, k_in, v_in, g_in, w_all, go, k_t, v_t,
    score, prob, q_t, out_t, inv_sum, out_all, row_dot, g_t, g_l, q_l, ds_buf, dq_t,
    g_out, o_out, o_in, o_rows, own_part, sib_out, sib_in, rs_out, rs_in, home, y_out, y_in,
    total, total_low, gs_in, done, dq_out, dk_out, dv_out,
    qkv_send, qkv_recv, w_send, w_recv, ws_send, ws_recv, g_send, g_recv, o_send, o_recv,
    sib_send, sib_recv, rs_send, rs_recv, y_send, y_recv, gs_send, gs_recv, gw_send, gw_recv,
    d_send, d_recv, local_sem,
):
    s = lax.axis_index("seq")
    d = lax.axis_index("dp")
    chip, core = d // 2, lax.rem(d, 2)
    y, x = chip // X, lax.rem(chip, X)
    length = n * rows
    chunks = length // CHUNK
    wide = 2 * rows
    half = HEAD_DIM
    columns = width // n
    batch = n // 2

    def ahead(base, i):
        return lax.rem(base + i, n)

    def behind(base, i):
        return lax.rem(base + n - i, n)

    def block(index, size):
        return pl.ds(pl.multiple_of(index * size, size), size)

    def remote(src, dst, send, recv, where):
        return pltpu.make_async_remote_copy(
            src_ref=src, dst_ref=dst, send_sem=send, recv_sem=recv,
            device_id=where, device_id_type=pl.DeviceIdType.MESH,
        )

    my_half = block(core, half)
    sibling = {"dp": 2 * chip + 1 - core}

    def chip_at(dy, dx):
        return lax.rem(y + dy, 2) * X + lax.rem(x + dx, X)

    def device_at(dy, dx):
        return {"dp": 2 * chip_at(dy, dx) + core}

    def qkv_copy(t, i):
        src, dst = ((k_ref, k_in), (v_ref, v_in), (q_ref, q_in))[t]
        peer = ahead(s, i)
        return remote(
            src.at[0, :, block(peer, LANES)], dst.at[i], qkv_send.at[t, i], qkv_recv.at[t, i], {"seq": peer}
        )

    def w_copy(slot):
        src = {7: 4, 5: 4, 2: 3, 6: 5}.get(slot)
        dy, dx = {3: (0, 1), 1: (0, 3), 4: (1, 0), 7: (0, 1), 5: (0, 3), 2: (0, 1), 6: (0, 3)}[slot]
        return remote(
            w_ref if src is None else w_all.at[src, my_half, :],
            w_all.at[slot, my_half, :], w_send.at[slot], w_recv.at[slot], device_at(dy, dx),
        )

    def ws_copy(slot):
        part = w_all.at[slot, my_half, :]
        return remote(w_ref if slot == 0 else part, part, ws_send.at[slot], ws_recv.at[slot], sibling)

    def g_copy(i):
        return remote(g_out.at[i], g_in.at[i], g_send.at[i], g_recv.at[i], {"seq": ahead(s, i)})

    def o_copy(i):
        return remote(o_out.at[i], o_in.at[i], o_send.at[i], o_recv.at[i], {"seq": behind(s, i)})

    def sib_copy(b):
        part = pl.ds(b * batch, batch)
        return remote(sib_out.at[part], sib_in.at[part], sib_send.at[b], sib_recv.at[b], sibling)

    def where_to(i):
        h = ahead(s, i)
        return lax.rem(h // X + y, 2), lax.rem(lax.rem(h, X) + X - x, X)

    def rs_copy(i):
        dy, dx = where_to(i)
        slot = dy * X + lax.rem(X - dx, X)
        return remote(rs_out.at[i], rs_in.at[slot], rs_send.at[i], rs_recv.at[slot], device_at(0, dx))

    def rs_arrival(slot):
        return remote(rs_out.at[0], rs_in.at[slot], rs_send.at[0], rs_recv.at[slot], device_at(0, 1))

    def y_copy():
        return remote(y_out, y_in, y_send.at[0], y_recv.at[0], device_at(1, 0))

    def gs_copy(i):
        peer = ahead(s, i)
        return remote(total_low.at[peer], gs_in.at[i], gs_send.at[i], gs_recv.at[i], {"seq": peer})

    def gw_copy(i):
        return remote(
            done, gw_ref.at[:, block(s, columns)], gw_send.at[i], gw_recv.at[i], {"seq": ahead(s, i)}
        )

    def d_copy(t, i):
        src = (dq_out, dk_out, dv_out)[t]
        dst = dqkv_ref.at[0, :, block(t * n + s, LANES)]
        return remote(src.at[i], dst, d_send.at[t, i], d_recv.at[t, i], {"seq": behind(s, i)})

    def each(first, step, last=n):
        def body(i, carry):
            step(i)
            return carry

        lax.fori_loop(first, last, body, 0)

    local = [
        pltpu.make_async_copy(k_ref.at[0, :, block(s, LANES)], k_in.at[0], local_sem.at[0]),
        pltpu.make_async_copy(v_ref.at[0, :, block(s, LANES)], v_in.at[0], local_sem.at[1]),
        pltpu.make_async_copy(q_ref.at[0, :, block(s, LANES)], q_in.at[0], local_sem.at[2]),
        pltpu.make_async_copy(w_ref, w_all.at[0, my_half, :], local_sem.at[3]),
        pltpu.make_async_copy(go_ref.at[0], go, local_sem.at[4]),
    ]
    for copy in local:
        copy.start()

    barrier = pltpu.get_barrier_semaphore()

    def greet(where):
        pl.semaphore_signal(barrier, inc=1, device_id=where, device_id_type=pl.DeviceIdType.MESH)

    each(1, lambda i: greet({"seq": ahead(s, i)}))
    for dx in range(1, X):
        greet(device_at(0, dx))
    greet(device_at(1, 0))
    greet(sibling)
    pl.semaphore_wait(barrier, n - 1 + X - 1 + 2)

    for slot in (4, 3, 1):
        w_copy(slot).start()
    for t in range(3):
        each(1, lambda i: qkv_copy(t, i).start())
    ws_copy(0).start()
    for copy in local:
        copy.wait()

    def turn(src, dst, i):
        dst[:, block(i, rows)] = src[i].astype(F32).T.astype(BF16)

    def arrive(t, src, dst, i):
        qkv_copy(t, i).wait_recv()
        turn(src, dst, i)

    def hand_on(slot, *nexts):
        w_copy(slot).wait_recv()
        for following in nexts:
            w_copy(following).start()
        ws_copy(slot).start()

    turn(k_in, k_t, 0)
    turn(v_in, v_t, 0)
    hand_on(4, 7, 5)
    each(1, functools.partial(arrive, 0, k_in, k_t))
    hand_on(3, 2)
    hand_on(1)
    each(1, functools.partial(arrive, 1, v_in, v_t))
    hand_on(5, 6)
    hand_on(7)

    k_rows = k_in.reshape(length, LANES)
    v_rows = v_in.reshape(length, LANES)

    def grad_attn(slot):
        ws_copy(slot).wait_recv()
        i = behind(chip_at(slot // X, slot % X), s)
        g = dot_nt(go[...], w_all[slot]).astype(BF16)

        @pl.when(i == 0)
        def _():
            g_in[0] = g

        @pl.when(i > 0)
        def _():
            g_out[i] = g
            g_copy(i).start()

    def weight_part(b):
        first = b * batch
        each(max(first, 1), lambda i: o_copy(i).wait_recv(), first + batch)
        for i in range(batch):
            o_rows[i * half : (i + 1) * half, :] = o_in[first + i, my_half, :]
            o_rows[(batch + i) * half : (batch + i + 1) * half, :] = o_in[first + i, block(1 - core, half), :]
        for c in range(n):
            cut = slice(c * columns, (c + 1) * columns)
            part = dot(o_rows[...], go[:, cut]).astype(BF16)
            own_part[first : first + batch, :, cut] = part[: batch * half].reshape(batch, half, columns)
            sib_out[first : first + batch, :, cut] = part[batch * half :].reshape(batch, half, columns)
        sib_copy(b).start()

    def share(b):
        sib_copy(b).wait_recv()

        def send(i):
            dy, dx = where_to(i)
            pair = own_part[i].astype(F32) + sib_in[i].astype(F32)

            @pl.when(dx == 0)
            def _():
                home[dy] = pair

            @pl.when(dx > 0)
            def _():
                rs_out[i] = pair.astype(BF16)
                rs_copy(i).start()

        each(b * batch, send, (b + 1) * batch)

    def row_sum():
        for slot in range(1, 2 * X):
            if slot != X:
                rs_arrival(slot).wait_recv()
        for c in range(n):
            cut = slice(c * columns, (c + 1) * columns)
            for dy in (1, 0):
                value = home[dy, :, cut]
                for dx in range(1, X):
                    value += rs_in[dy * X + dx, :, cut].astype(F32)
                if dy:
                    y_out[:, cut] = value.astype(BF16)
                else:
                    total[c] = value
        y_copy().start()

    def chip_sum():
        y_copy().wait_recv()
        for c in range(n):
            value = total[c] + y_in[:, c * columns : (c + 1) * columns].astype(F32)
            total[c] = value
            total_low[c] = value.astype(BF16)
        each(1, lambda i: gs_copy(i).start())

    def weight_out():
        each(1, lambda i: gs_copy(i).wait_recv())
        value = total[s]
        for i in range(1, n):
            value += gs_in[i].astype(F32)
        done[...] = value
        each(1, lambda i: gw_copy(i).start())
        gw_ref[:, block(s, columns)] = value

    def forward(i, carry):
        @pl.when(i > 0)
        def _():
            qkv_copy(2, i).wait_recv()

        queries = split_heads(q_in[i].astype(F32).T)
        q_t[...] = queries.astype(BF16)

        def score_chunk(c, top):
            keys = block(c, CHUNK)
            value = dot(k_rows[keys, :], q_t[...])
            score[keys, :] = value
            return jnp.maximum(top, jnp.max(value.reshape(CHUNK // 8, 8, wide), axis=0))

        top = lax.fori_loop(0, chunks, score_chunk, jnp.full((8, wide), -jnp.inf, F32), unroll=True)
        top = jnp.max(top, axis=0, keepdims=True)
        out_t[...] = jnp.zeros_like(out_t)

        def prob_chunk(c, norm):
            keys = block(c, CHUNK)
            p = jnp.exp2((score[keys, :] - top) * EXP_SCALE)
            low = p.astype(BF16)
            prob[keys, block(i, wide)] = low
            out_t[...] += dot(v_t[:, keys], low)
            return norm + jnp.sum(p.reshape(CHUNK // 8, 8, wide), axis=0)

        norm = lax.fori_loop(0, chunks, prob_chunk, jnp.zeros((8, wide), F32), unroll=True)
        inverse = 1.0 / jnp.sum(norm, axis=0, keepdims=True)
        inv_sum[i] = jnp.broadcast_to(inverse, (8, wide))
        q_l[block(i, wide), :] = (split_heads(q_in[i].astype(F32).T) * (inverse * SCALING)).T.astype(BF16)
        merged = merge_heads(out_t[...] * inverse)
        out_all[i] = merged

        @pl.when(i == 0)
        def _():
            o_in[0] = merged.astype(BF16)

        @pl.when(i > 0)
        def _():
            o_out[i] = merged.astype(BF16)
            o_copy(i).start()

        @pl.when(i == 0)
        def _():
            grad_attn(0)
            grad_attn(4)

        @pl.when(i == 1)
        def _():
            hand_on(2)
            hand_on(6)
            grad_attn(3)
            grad_attn(1)

        @pl.when(i == 2)
        def _():
            grad_attn(5)
            grad_attn(7)

        @pl.when(i == 3)
        def _():
            grad_attn(2)
            grad_attn(6)

        @pl.when(i == batch)
        def _():
            weight_part(0)

        @pl.when(i == batch + 1)
        def _():
            share(0)

        return carry

    lax.fori_loop(0, n, forward, 0)
    weight_part(1)

    def prepare(i, carry):
        @pl.when(i > 0)
        def _():
            g_copy(i).wait_recv()

        g = g_in[i].astype(F32).T
        g_split = split_heads(g)
        g_t[:, block(i, wide)] = g_split.astype(BF16)
        g_l[block(i, wide), :] = (g_split * inv_sum[i, 0:1, :]).T.astype(BF16)
        product = out_all[i] * g
        both = jnp.concatenate(
            [
                jnp.sum(product[:half], axis=0, keepdims=True),
                jnp.sum(product[half:], axis=0, keepdims=True),
            ],
            axis=1,
        )
        row_dot[i] = jnp.broadcast_to(both, (8, wide))
        return carry

    lax.fori_loop(0, n, prepare, 0)
    share(1)
    dq_t[...] = jnp.zeros_like(dq_t)

    def backward(j, carry):
        keys = block(j, rows)

        def grad_chunk(i, carry):
            cut = block(i, wide)
            grad_prob = dot(v_rows[keys, :], g_t[:, cut])
            grad_score = (prob[keys, cut].astype(F32) * (grad_prob - row_dot[i, 0:1, :])).astype(BF16)
            ds_buf[:, cut] = grad_score
            dq_t[:, cut] += dot(k_t[:, keys], grad_score)
            return carry

        lax.fori_loop(0, n, grad_chunk, 0, unroll=True)
        grad_v = dot(prob[keys, :], g_l[...]).astype(BF16)
        grad_k = dot(ds_buf[...], q_l[...]).astype(BF16)

        @pl.when(j == 0)
        def _():
            dqkv_ref[0, :, block(n + s, LANES)] = grad_k
            dqkv_ref[0, :, block(2 * n + s, LANES)] = grad_v

        @pl.when(j > 0)
        def _():
            dk_out[j] = grad_k
            d_copy(1, j).start()
            dv_out[j] = grad_v
            d_copy(2, j).start()

        @pl.when(j == n - 4)
        def _():
            row_sum()

        @pl.when(j == n - 2)
        def _():
            chip_sum()

        return carry

    lax.fori_loop(0, n, backward, 0)

    def grad_q(i):
        return merge_heads(dq_t[:, block(i, wide)] * (inv_sum[i, 0:1, :] * SCALING)).T.astype(BF16)

    def finish(i):
        dq_out[i] = grad_q(i)
        d_copy(0, i).start()

    each(1, finish)
    dqkv_ref[0, :, block(s, LANES)] = grad_q(0)
    weight_out()

    def arrivals(i):
        for t in range(3):
            d_copy(t, i).wait_recv()
        gw_copy(i).wait_recv()

    each(1, arrivals)

    def sent(i):
        for t in range(3):
            qkv_copy(t, i).wait_send()
            d_copy(t, i).wait_send()
        g_copy(i).wait_send()
        o_copy(i).wait_send()
        gs_copy(i).wait_send()
        gw_copy(i).wait_send()

    each(1, sent)
    for slot in range(n):
        if slot:
            w_copy(slot).wait_send()
        ws_copy(slot).wait_send()
    sib_copy(0).wait_send()
    sib_copy(1).wait_send()
    y_copy().wait_send()

    def rs_sent(i):
        @pl.when(where_to(i)[1] > 0)
        def _():
            rs_copy(i).wait_send()

    each(0, rs_sent)


def on_device(n, queries, keys, values, out_proj, grad_out):
    rows, features = queries.shape[1:]
    share_rows, width = out_proj.shape
    length = n * rows
    wide = 2 * rows
    columns = width // n
    vmem = pltpu.VMEM
    dma = pltpu.SemaphoreType.DMA
    flat = vmem((n, rows, LANES), BF16)
    turned = vmem((n, LANES, rows), BF16)
    shares = vmem((n, HEAD_DIM, width), BF16)
    return pl.pallas_call(
        functools.partial(kernel, n, rows, width),
        out_shape=(
            jax.ShapeDtypeStruct((1, rows, 3 * features), BF16),
            jax.ShapeDtypeStruct((share_rows, width), F32),
        ),
        in_specs=[pl.BlockSpec(memory_space=pl.ANY)] * 5,
        out_specs=[pl.BlockSpec(memory_space=vmem)] * 2,
        scratch_shapes=[
            flat, flat, flat, flat,
            vmem((n, LANES, width), BF16),
            vmem((rows, width), BF16),
            vmem((LANES, length), BF16),
            vmem((LANES, length), BF16),
            vmem((length, wide), F32),
            vmem((length, n * wide), BF16),
            vmem((LANES, wide), BF16),
            vmem((LANES, wide), F32),
            vmem((n, 8, wide), F32),
            vmem((n, LANES, rows), F32),
            vmem((n, 8, wide), F32),
            vmem((LANES, n * wide), BF16),
            vmem((n * wide, LANES), BF16),
            vmem((n * wide, LANES), BF16),
            vmem((rows, n * wide), BF16),
            vmem((LANES, n * wide), F32),
            flat, turned, turned,
            vmem((n * HEAD_DIM, rows), BF16),
            shares, shares, shares, shares, shares,
            vmem((2, HEAD_DIM, width), F32),
            vmem((HEAD_DIM, width), BF16),
            vmem((HEAD_DIM, width), BF16),
            vmem((n, HEAD_DIM, columns), F32),
            vmem((n, HEAD_DIM, columns), BF16),
            vmem((n, HEAD_DIM, columns), BF16),
            vmem((HEAD_DIM, columns), F32),
            flat, flat, flat,
            dma((3, n)), dma((3, n)),
            dma((n,)), dma((n,)), dma((n,)), dma((n,)),
            dma((n,)), dma((n,)), dma((n,)), dma((n,)),
            dma((2,)), dma((2,)), dma((n,)), dma((n,)), dma((1,)), dma((1,)),
            dma((n,)), dma((n,)), dma((n,)), dma((n,)),
            dma((3, n)), dma((3, n)), dma((5,)),
        ],
        compiler_params=pltpu.CompilerParams(
            collective_id=0, has_side_effects=True, vmem_limit_bytes=60 << 20
        ),
    )(queries, keys, values, out_proj, grad_out)


def solution(mesh):
    return jax.shard_map(
        functools.partial(on_device, mesh.shape["seq"]),
        mesh=mesh,
        in_specs=(
            P("dp", "seq", None),
            P("dp", "seq", None),
            P("dp", "seq", None),
            P("dp", None),
            P("dp", "seq", None),
        ),
        out_specs=(P("dp", "seq", None), P("dp", None)),
        check_vma=False,
    )
```

```python
import functools
import math

import jax
import jax.numpy as jnp
from jax import lax
from jax.experimental import pallas as pl
from jax.experimental.pallas import tpu as pltpu
from jax.sharding import PartitionSpec as P

HEAD_DIM = 64
LANES = 2 * HEAD_DIM
X = 4
Z = 4
SPAN = 2
EARLY = 4
CHUNK = 512
SCALING = HEAD_DIM ** (-0.5)
EXP_SCALE = SCALING * math.log2(math.e)
F32 = jnp.float32
BF16 = jnp.bfloat16


def dot(a, b):
    return jnp.dot(a, b, preferred_element_type=F32)


def dot_nt(a, b):
    return lax.dot_general(a, b, (((1,), (1,)), ((), ())), preferred_element_type=F32)


def split_heads(columns):
    row = lax.broadcasted_iota(jnp.int32, columns.shape, 0)
    zeros = jnp.zeros_like(columns)
    return jnp.concatenate(
        [jnp.where(row < HEAD_DIM, columns, zeros), jnp.where(row < HEAD_DIM, zeros, columns)], axis=1
    )


def merge_heads(wide):
    rows = wide.shape[1] // 2
    first, second = wide[:, :rows], wide[:, rows:]
    row = lax.broadcasted_iota(jnp.int32, first.shape, 0)
    return jnp.where(row < HEAD_DIM, first, second)


def kernel(
    n, rows, width,
    q_ref, k_ref, v_ref, w_ref, go_ref, dqkv_ref, gw_ref,
    q_in, k_in, v_in, g_in, w_all, go, go_t, k_t, v_t,
    score, prob, q_t, out_t, inv_sum, out_all, row_dot, g_t, g_l, q_l, ds_buf, dq_t,
    g_out, o_out, o_in, o_rows, own_part, sib_out, sib_in, rs_out, rs_in, home,
    total, zs_out, zs_in, ys_out, ys_in, done, dq_out, dk_out, dv_out,
    qkv_send, qkv_recv, w_send, w_recv, ws_send, ws_recv, g_send, g_recv, o_send, o_recv,
    sib_send, sib_recv, rs_send, rs_recv, zs_send, zs_recv, ys_send, ys_recv, gw_send, gw_recv,
    d_send, d_recv, local_sem,
):
    s = lax.axis_index("seq")
    d = lax.axis_index("dp")
    chip, core = d // 2, lax.rem(d, 2)
    y, x = chip // X, lax.rem(chip, X)
    z, y_hi = s // 2, lax.rem(s, 2)
    quarter = width // Z
    length = n * rows
    chunks = length // CHUNK
    wide = 2 * rows
    half = HEAD_DIM
    columns = width // n
    batch = n // 2
    span = SPAN * rows
    steps = n // SPAN

    def ahead(base, i):
        return lax.rem(base + i, n)

    def behind(base, i):
        return lax.rem(base + n - i, n)

    def block(index, size):
        return pl.ds(pl.multiple_of(index * size, size), size)

    def remote(src, dst, send, recv, where):
        return pltpu.make_async_remote_copy(
            src_ref=src, dst_ref=dst, send_sem=send, recv_sem=recv,
            device_id=where, device_id_type=pl.DeviceIdType.MESH,
        )

    my_half = block(core, half)
    sibling = {"dp": 2 * chip + 1 - core}

    def chip_at(dy, dx):
        return lax.rem(y + dy, 2) * X + lax.rem(x + dx, X)

    def device_at(dy, dx):
        return {"dp": 2 * chip_at(dy, dx) + core}

    def qkv_copy(t, i):
        src, dst = ((k_ref, k_in), (v_ref, v_in), (q_ref, q_in))[t]
        peer = ahead(s, i)
        return remote(
            src.at[0, :, block(peer, LANES)], dst.at[i], qkv_send.at[t, i], qkv_recv.at[t, i], {"seq": peer}
        )

    def w_copy(slot):
        src = {7: 4, 5: 4, 2: 3, 6: 5}.get(slot)
        dy, dx = {3: (0, 1), 1: (0, 3), 4: (1, 0), 7: (0, 1), 5: (0, 3), 2: (0, 1), 6: (0, 3)}[slot]
        return remote(
            w_ref if src is None else w_all.at[src, my_half, :],
            w_all.at[slot, my_half, :], w_send.at[slot], w_recv.at[slot], device_at(dy, dx),
        )

    def ws_copy(slot):
        part = w_all.at[slot, my_half, :]
        return remote(w_ref if slot == 0 else part, part, ws_send.at[slot], ws_recv.at[slot], sibling)

    def g_copy(i):
        return remote(g_out.at[i], g_in.at[i], g_send.at[i], g_recv.at[i], {"seq": ahead(s, i)})

    def o_copy(i):
        return remote(o_out.at[i], o_in.at[i], o_send.at[i], o_recv.at[i], {"seq": behind(s, i)})

    def sib_copy(b):
        part = pl.ds(b * batch, batch)
        return remote(sib_out.at[part], sib_in.at[part], sib_send.at[b], sib_recv.at[b], sibling)

    def where_to(i):
        h = ahead(s, i)
        return lax.rem(h // X + y, 2), lax.rem(lax.rem(h, X) + X - x, X)

    def rs_copy(i):
        dy, dx = where_to(i)
        slot = dy * X + lax.rem(X - dx, X)
        return remote(rs_out.at[i], rs_in.at[slot], rs_send.at[i], rs_recv.at[slot], device_at(0, dx))

    def rs_arrival(slot):
        return remote(rs_out.at[0], rs_in.at[slot], rs_send.at[0], rs_recv.at[slot], device_at(0, 1))

    def zs_copy(k):
        to = lax.rem(z + k, Z)
        return remote(
            zs_out.at[to], zs_in.at[k], zs_send.at[k], zs_recv.at[k], {"seq": 2 * to + y_hi}
        )

    def ys_copy(k):
        dy, dh = ((1, 0), (1, 1), (0, 1))[k]
        where = {
            "seq": 2 * z + lax.rem(y_hi + dh, 2),
            "dp": 2 * chip_at(dy, 0) + core,
        }
        return remote(ys_out.at[dy], ys_in.at[2 * y_hi + y], ys_send.at[k], ys_recv.at[k], where)

    def gw_copy(k):
        to = lax.rem(z + k, Z)
        return remote(
            done, gw_ref.at[:, block(z, quarter)], gw_send.at[k], gw_recv.at[k], {"seq": 2 * to + y_hi}
        )

    def d_copy(t, i):
        src = (dq_out, dk_out, dv_out)[t]
        dst = dqkv_ref.at[0, :, block(t * n + s, LANES)]
        return remote(src.at[i], dst, d_send.at[t, i], d_recv.at[t, i], {"seq": behind(s, i)})

    def each(first, step, last=n):
        def body(i, carry):
            step(i)
            return carry

        lax.fori_loop(first, last, body, 0)

    local = [
        pltpu.make_async_copy(k_ref.at[0, :, block(s, LANES)], k_in.at[0], local_sem.at[0]),
        pltpu.make_async_copy(v_ref.at[0, :, block(s, LANES)], v_in.at[0], local_sem.at[1]),
        pltpu.make_async_copy(q_ref.at[0, :, block(s, LANES)], q_in.at[0], local_sem.at[2]),
        pltpu.make_async_copy(w_ref, w_all.at[0, my_half, :], local_sem.at[3]),
        pltpu.make_async_copy(go_ref.at[0], go, local_sem.at[4]),
    ]
    for copy in local:
        copy.start()

    barrier = pltpu.get_barrier_semaphore()

    def greet(where):
        pl.semaphore_signal(barrier, inc=1, device_id=where, device_id_type=pl.DeviceIdType.MESH)

    each(1, lambda i: greet({"seq": ahead(s, i)}))
    for dx in range(1, X):
        greet(device_at(0, dx))
    greet(device_at(1, 0))
    greet({"seq": 2 * z + 1 - y_hi, **device_at(1, 0)})
    greet(sibling)
    pl.semaphore_wait(barrier, n - 1 + X - 1 + 3)

    for slot in (4, 3, 1):
        w_copy(slot).start()
    for t in (0, 2, 1):
        each(1, lambda i: qkv_copy(t, i).start())
    ws_copy(0).start()
    for copy in local:
        copy.wait()
    for c in range(n):
        cut = slice(c * columns, (c + 1) * columns)
        go_t[cut, :] = go[:, cut].astype(F32).T.astype(BF16)

    def turn(src, dst, i):
        dst[:, block(i, rows)] = src[i].astype(F32).T.astype(BF16)

    def hand_on(slot, *nexts):
        w_copy(slot).wait_recv()
        for following in nexts:
            w_copy(following).start()
        ws_copy(slot).start()

    hand_on(4, 7, 5)
    each(1, lambda i: qkv_copy(0, i).wait_recv())

    k_rows = k_in.reshape(length, LANES)
    v_rows = v_in.reshape(length, LANES)

    def grad_attn(*slots):
        for slot in slots:
            ws_copy(slot).wait_recv()
        both = dot(jnp.concatenate([w_all[slot] for slot in slots], axis=0), go_t[...]).astype(BF16)
        for at, slot in enumerate(slots):
            i = behind(chip_at(slot // X, slot % X), s)
            g = both[at * LANES : (at + 1) * LANES]

            @pl.when(i == 0)
            def _():
                g_in[0] = g

            @pl.when(i > 0)
            def _():
                g_out[i] = g
                g_copy(i).start()

    def weight_part(b):
        first = b * batch
        each(max(first, 1), lambda i: o_copy(i).wait_recv(), first + batch)
        for i in range(batch):
            o_rows[i * half : (i + 1) * half, :] = o_in[first + i, my_half, :]
            o_rows[(batch + i) * half : (batch + i + 1) * half, :] = o_in[first + i, block(1 - core, half), :]
        for c in range(n):
            cut = slice(c * columns, (c + 1) * columns)
            part = dot(o_rows[...], go[:, cut]).astype(BF16)
            own_part[first : first + batch, :, cut] = part[: batch * half].reshape(batch, half, columns)
            sib_out[first : first + batch, :, cut] = part[batch * half :].reshape(batch, half, columns)
        sib_copy(b).start()

    def share(b):
        sib_copy(b).wait_recv()

        def send(i):
            dy, dx = where_to(i)
            pair = own_part[i].astype(F32) + sib_in[i].astype(F32)

            @pl.when(dx == 0)
            def _():
                home[dy] = pair

            @pl.when(dx > 0)
            def _():
                rs_out[i] = pair.astype(BF16)
                rs_copy(i).start()

        each(b * batch, send, (b + 1) * batch)

    def row_sum():
        for slot in range(1, 2 * X):
            if slot != X:
                rs_arrival(slot).wait_recv()
        for c in range(Z):
            cut = slice(c * quarter, (c + 1) * quarter)
            for dy in range(2):
                value = home[dy, :, cut]
                for dx in range(1, X):
                    value += rs_in[dy * X + dx, :, cut].astype(F32)
                total[c, dy] = value
                zs_out[c, dy] = value.astype(BF16)
        for k in range(1, Z):
            zs_copy(k).start()

    def patch_sum():
        for k in range(1, Z):
            zs_copy(k).wait_recv()
        for dy in range(2):
            value = total[z, dy]
            for k in range(1, Z):
                value += zs_in[k, dy].astype(F32)
            ys_out[dy] = value.astype(BF16)
        for k in range(3):
            ys_copy(k).start()
        ys_in[2 * y_hi + y] = ys_out[0]

    def weight_out():
        for k in range(3):
            ys_copy(k).wait_recv()
        value = ys_in[0].astype(F32)
        for at in range(1, 4):
            value += ys_in[at].astype(F32)
        done[...] = value
        for k in range(1, Z):
            gw_copy(k).start()
        gw_ref[:, block(z, quarter)] = value

    def column(value):
        return jnp.broadcast_to(value, (8, wide)).T[:, 0:1]

    def scaled_rows(natural, scale):
        lane = lax.broadcasted_iota(jnp.int32, natural.shape, 1)
        first = jnp.where(lane < half, natural * scale[:rows], 0.0)
        second = jnp.where(lane < half, 0.0, natural * scale[rows:])
        return jnp.concatenate([first, second], axis=0).astype(BF16)

    def probs(i, with_out):
        @pl.when(i > 0)
        def _():
            qkv_copy(2, i).wait_recv()

        q = q_in[i].astype(F32)
        q_t[...] = split_heads(q.T).astype(BF16)

        def score_chunk(c, top):
            keys = block(c, CHUNK)
            value = dot(k_rows[keys, :], q_t[...])
            score[keys, :] = value
            return jnp.maximum(top, jnp.max(value.reshape(CHUNK // 8, 8, wide), axis=0))

        top = lax.fori_loop(0, chunks, score_chunk, jnp.full((8, wide), -jnp.inf, F32), unroll=True)
        top = jnp.max(top, axis=0, keepdims=True)
        if with_out:
            out_t[...] = jnp.zeros_like(out_t)

        def prob_chunk(c, norm):
            keys = block(c, CHUNK)
            p = jnp.exp2((score[keys, :] - top) * EXP_SCALE)
            low = p.astype(BF16)
            prob[keys, block(i, wide)] = low
            if with_out:
                out_t[...] += dot(v_t[:, keys], low)
            return norm + jnp.sum(p.reshape(CHUNK // 8, 8, wide), axis=0)

        norm = lax.fori_loop(0, chunks, prob_chunk, jnp.zeros((8, wide), F32), unroll=True)
        inverse = 1.0 / jnp.sum(norm, axis=0, keepdims=True)
        inv_sum[i] = jnp.broadcast_to(inverse, (8, wide))
        q_l[block(i, wide), :] = scaled_rows(q, column(inverse * SCALING))
        if with_out:
            send_out(i, out_t[...] * inverse)

    def send_out(i, wide_out):
        merged = merge_heads(wide_out)
        out_all[i] = merged

        @pl.when(i == 0)
        def _():
            o_in[0] = merged.astype(BF16)

        @pl.when(i > 0)
        def _():
            o_out[i] = merged.astype(BF16)
            o_copy(i).start()

    def early(i, carry):
        probs(i, False)

        @pl.when(i == 0)
        def _():
            hand_on(3, 2)
            hand_on(1)
            grad_attn(0, 4)

        @pl.when(i == 1)
        def _():
            hand_on(5, 6)
            grad_attn(3, 1)

        @pl.when(i == 2)
        def _():
            hand_on(7)

        return carry

    def late(i, carry):
        probs(i, True)

        @pl.when(i == EARLY)
        def _():
            grad_attn(2, 6)

        @pl.when(i == batch + 1)
        def _():
            weight_part(0)

        @pl.when(i == batch + 2)
        def _():
            share(0)

        return carry

    lax.fori_loop(0, EARLY, early, 0)
    turn(k_in, k_t, 0)
    each(1, lambda i: turn(k_in, k_t, i))
    grad_attn(5, 7)
    turn(v_in, v_t, 0)

    def arrive(i):
        qkv_copy(1, i).wait_recv()
        turn(v_in, v_t, i)

    each(1, arrive)
    each(0, lambda i: send_out(i, dot(v_t[...], prob[:, block(i, wide)]) * inv_sum[i, 0:1, :]), EARLY)
    hand_on(2)
    hand_on(6)
    lax.fori_loop(EARLY, n, late, 0)

    def prepare(i, carry):
        @pl.when(i > 0)
        def _():
            g_copy(i).wait_recv()

        g = g_in[i].astype(F32)
        g_t[:, block(i, wide)] = split_heads(g).astype(BF16)
        g_l[block(i, wide), :] = scaled_rows(g.T, column(inv_sum[i, 0:1, :]))
        product = out_all[i] * g
        both = jnp.concatenate(
            [
                jnp.sum(product[:half], axis=0, keepdims=True),
                jnp.sum(product[half:], axis=0, keepdims=True),
            ],
            axis=1,
        )
        row_dot[i] = jnp.broadcast_to(both, (8, wide))
        return carry

    lax.fori_loop(0, n, prepare, 0)
    weight_part(1)
    dq_t[...] = jnp.zeros_like(dq_t)
    share(1)

    def grad_q(i):
        return merge_heads(dq_t[:, block(i, wide)] * (inv_sum[i, 0:1, :] * SCALING)).T.astype(BF16)

    def backward(j, last):
        keys = block(j, span)

        def grad_chunk(i):
            cut = block(i, wide)
            grad_prob = dot(v_rows[keys, :], g_t[:, cut])
            grad_score = (prob[keys, cut].astype(F32) * (grad_prob - row_dot[i, 0:1, :])).astype(BF16)
            ds_buf[:, cut] = grad_score
            dq_t[:, cut] += dot(k_t[:, keys], grad_score)
            if last:
                dq_out[i] = grad_q(i)
                if i:
                    d_copy(0, i).start()

        for i in range(n):
            grad_chunk(i)
        grad_v = dot(prob[keys, :], g_l[...]).astype(BF16)
        grad_k = dot(ds_buf[...], q_l[...]).astype(BF16)

        for part in range(SPAN):
            i = j * SPAN + part
            cut = slice(part * rows, (part + 1) * rows)
            dk_out[i] = grad_k[cut]
            dv_out[i] = grad_v[cut]

            @pl.when(i > 0)
            def _():
                d_copy(1, i).start()
                d_copy(2, i).start()

    def backward_step(j, carry):
        backward(j, False)

        @pl.when(j == steps - 3)
        def _():
            row_sum()

        @pl.when(j == steps - 2)
        def _():
            patch_sum()

        return carry

    lax.fori_loop(0, steps - 1, backward_step, 0)
    backward(steps - 1, True)
    weight_out()
    for t in range(3):
        dqkv_ref[0, :, block(t * n + s, LANES)] = (dq_out, dk_out, dv_out)[t][0]

    def arrivals(i):
        for t in range(3):
            d_copy(t, i).wait_recv()

    each(1, arrivals)

    def sent(i):
        for t in range(3):
            qkv_copy(t, i).wait_send()
            d_copy(t, i).wait_send()
        g_copy(i).wait_send()
        o_copy(i).wait_send()

    each(1, sent)
    for slot in range(n):
        if slot:
            w_copy(slot).wait_send()
        ws_copy(slot).wait_send()
    sib_copy(0).wait_send()
    sib_copy(1).wait_send()
    for k in range(3):
        ys_copy(k).wait_send()
        zs_copy(k + 1).wait_send()
        gw_copy(k + 1).wait_send()
        gw_copy(k + 1).wait_recv()

    def rs_sent(i):
        @pl.when(where_to(i)[1] > 0)
        def _():
            rs_copy(i).wait_send()

    each(0, rs_sent)


def on_device(n, queries, keys, values, out_proj, grad_out):
    rows, features = queries.shape[1:]
    share_rows, width = out_proj.shape
    length = n * rows
    wide = 2 * rows
    columns = width // n
    vmem = pltpu.VMEM
    dma = pltpu.SemaphoreType.DMA
    flat = vmem((n, rows, LANES), BF16)
    turned = vmem((n, LANES, rows), BF16)
    shares = vmem((n, HEAD_DIM, width), BF16)
    return pl.pallas_call(
        functools.partial(kernel, n, rows, width),
        out_shape=(
            vmem((1, rows, 3 * features), BF16),
            vmem((share_rows, width), F32),
        ),
        in_specs=[pl.BlockSpec(memory_space=pl.ANY)] * 5,
        out_specs=[pl.BlockSpec(memory_space=vmem)] * 2,
        scratch_shapes=[
            flat, flat, flat, turned,
            vmem((n, LANES, width), BF16),
            vmem((rows, width), BF16),
            vmem((width, rows), BF16),
            vmem((LANES, length), BF16),
            vmem((LANES, length), BF16),
            vmem((length, wide), F32),
            vmem((length, n * wide), BF16),
            vmem((LANES, wide), BF16),
            vmem((LANES, wide), F32),
            vmem((n, 8, wide), F32),
            vmem((n, LANES, rows), F32),
            vmem((n, 8, wide), F32),
            vmem((LANES, n * wide), BF16),
            vmem((n * wide, LANES), BF16),
            vmem((n * wide, LANES), BF16),
            vmem((SPAN * rows, n * wide), BF16),
            vmem((LANES, n * wide), F32),
            turned, turned, turned,
            vmem((n * HEAD_DIM, rows), BF16),
            shares, shares, shares, shares, shares,
            vmem((2, HEAD_DIM, width), F32),
            vmem((Z, 2, HEAD_DIM, width // Z), F32),
            vmem((Z, 2, HEAD_DIM, width // Z), BF16),
            vmem((Z, 2, HEAD_DIM, width // Z), BF16),
            vmem((2, HEAD_DIM, width // Z), BF16),
            vmem((4, HEAD_DIM, width // Z), BF16),
            vmem((HEAD_DIM, width // Z), F32),
            flat, flat, flat,
            dma((3, n)), dma((3, n)),
            dma((n,)), dma((n,)), dma((n,)), dma((n,)),
            dma((n,)), dma((n,)), dma((n,)), dma((n,)),
            dma((2,)), dma((2,)), dma((n,)), dma((n,)),
            dma((Z,)), dma((Z,)), dma((3,)), dma((3,)), dma((Z,)), dma((Z,)),
            dma((3, n)), dma((3, n)), dma((5,)),
        ],
        compiler_params=pltpu.CompilerParams(
            collective_id=0, has_side_effects=True, vmem_limit_bytes=60 << 20
        ),
    )(queries, keys, values, out_proj, grad_out)


def solution(mesh):
    return jax.shard_map(
        functools.partial(on_device, mesh.shape["seq"]),
        mesh=mesh,
        in_specs=(
            P("dp", "seq", None),
            P("dp", "seq", None),
            P("dp", "seq", None),
            P("dp", None),
            P("dp", "seq", None),
        ),
        out_specs=(P("dp", "seq", None), P("dp", None)),
        check_vma=False,
    )
```

```python
import functools
import math

import jax
import jax.numpy as jnp
from jax import lax
from jax.experimental import pallas as pl
from jax.experimental.pallas import tpu as pltpu
from jax.sharding import PartitionSpec as P

HEAD_DIM = 64
LANES = 2 * HEAD_DIM
X = 4
Z = 4
SPAN = 2
EARLY = 4
CHUNK = 512
SCALING = HEAD_DIM ** (-0.5)
EXP_SCALE = SCALING * math.log2(math.e)
F32 = jnp.float32
BF16 = jnp.bfloat16


def dot(a, b):
    return jnp.dot(a, b, preferred_element_type=F32)


def dot_nt(a, b):
    return lax.dot_general(a, b, (((1,), (1,)), ((), ())), preferred_element_type=F32)


def split_heads(columns):
    row = lax.broadcasted_iota(jnp.int32, columns.shape, 0)
    zeros = jnp.zeros_like(columns)
    return jnp.concatenate(
        [jnp.where(row < HEAD_DIM, columns, zeros), jnp.where(row < HEAD_DIM, zeros, columns)], axis=1
    )


def merge_heads(wide):
    rows = wide.shape[1] // 2
    first, second = wide[:, :rows], wide[:, rows:]
    row = lax.broadcasted_iota(jnp.int32, first.shape, 0)
    return jnp.where(row < HEAD_DIM, first, second)


def kernel(
    n, rows, width,
    q_ref, k_ref, v_ref, w_ref, go_ref, dqkv_ref, gw_ref,
    q_in, k_in, v_in, g_in, w_all, go, go_t, k_t, v_t,
    score, prob, q_t, out_t, inv_sum, out_all, row_dot, g_t, g_l, q_l, ds_buf, dq_t,
    g_out, o_out, o_in, o_rows, own_part, sib_out, sib_in, rs_out, rs_in, home,
    total, zs_out, zs_in, ys_out, ys_in, done, gw_in, dq_out, dk_out, dv_out,
    qkv_send, qkv_recv, w_send, w_recv, ws_send, ws_recv, g_send, g_recv, o_send, o_recv,
    sib_send, sib_recv, rs_send, rs_recv, zs_send, zs_recv, ys_send, ys_recv, gw_send, gw_recv,
    d_send, d_recv, local_sem,
):
    s = lax.axis_index("seq")
    d = lax.axis_index("dp")
    chip, core = d // 2, lax.rem(d, 2)
    y, x = chip // X, lax.rem(chip, X)
    z, y_hi = s // 2, lax.rem(s, 2)
    quarter = width // Z
    length = n * rows
    chunks = length // CHUNK
    wide = 2 * rows
    half = HEAD_DIM
    columns = width // n
    batch = n // 2
    span = SPAN * rows
    steps = n // SPAN

    def ahead(base, i):
        return lax.rem(base + i, n)

    def behind(base, i):
        return lax.rem(base + n - i, n)

    def block(index, size):
        return pl.ds(pl.multiple_of(index * size, size), size)

    def remote(src, dst, send, recv, where):
        return pltpu.make_async_remote_copy(
            src_ref=src, dst_ref=dst, send_sem=send, recv_sem=recv,
            device_id=where, device_id_type=pl.DeviceIdType.MESH,
        )

    my_half = block(core, half)
    sibling = {"dp": 2 * chip + 1 - core}

    def chip_at(dy, dx):
        return lax.rem(y + dy, 2) * X + lax.rem(x + dx, X)

    def device_at(dy, dx):
        return {"dp": 2 * chip_at(dy, dx) + core}

    def qkv_copy(t, i):
        src, dst = ((k_ref, k_in), (v_ref, v_in), (q_ref, q_in))[t]
        peer = ahead(s, i)
        return remote(
            src.at[0, :, block(peer, LANES)], dst.at[i], qkv_send.at[t, i], qkv_recv.at[t, i], {"seq": peer}
        )

    def w_copy(slot):
        src = {7: 4, 5: 4, 2: 3, 6: 5}.get(slot)
        dy, dx = {3: (0, 1), 1: (0, 3), 4: (1, 0), 7: (0, 1), 5: (0, 3), 2: (0, 1), 6: (0, 3)}[slot]
        return remote(
            w_ref if src is None else w_all.at[src, my_half, :],
            w_all.at[slot, my_half, :], w_send.at[slot], w_recv.at[slot], device_at(dy, dx),
        )

    def ws_copy(slot):
        part = w_all.at[slot, my_half, :]
        return remote(w_ref if slot == 0 else part, part, ws_send.at[slot], ws_recv.at[slot], sibling)

    def g_copy(i):
        return remote(g_out.at[i], g_in.at[i], g_send.at[i], g_recv.at[i], {"seq": ahead(s, i)})

    def o_copy(i):
        return remote(o_out.at[i], o_in.at[i], o_send.at[i], o_recv.at[i], {"seq": behind(s, i)})

    def sib_copy(b):
        part = pl.ds(b * batch, batch)
        return remote(sib_out.at[part], sib_in.at[part], sib_send.at[b], sib_recv.at[b], sibling)

    def where_to(i):
        h = ahead(s, i)
        return lax.rem(h // X + y, 2), lax.rem(lax.rem(h, X) + X - x, X)

    def rs_copy(i):
        dy, dx = where_to(i)
        slot = dy * X + lax.rem(X - dx, X)
        return remote(rs_out.at[i], rs_in.at[slot], rs_send.at[i], rs_recv.at[slot], device_at(0, dx))

    def rs_arrival(slot):
        return remote(rs_out.at[0], rs_in.at[slot], rs_send.at[0], rs_recv.at[slot], device_at(0, 1))

    def zs_copy(k):
        to = lax.rem(z + k, Z)
        return remote(
            zs_out.at[to], zs_in.at[k], zs_send.at[k], zs_recv.at[k], {"seq": 2 * to + y_hi}
        )

    def ys_copy(k):
        dy, dh = ((1, 0), (1, 1), (0, 1))[k]
        where = {
            "seq": 2 * z + lax.rem(y_hi + dh, 2),
            "dp": 2 * chip_at(dy, 0) + core,
        }
        return remote(ys_out.at[dy], ys_in.at[2 * y_hi + y], ys_send.at[k], ys_recv.at[k], where)

    def gw_copy(k):
        to = lax.rem(z + k, Z)
        return remote(
            done, gw_in.at[k], gw_send.at[k], gw_recv.at[k], {"seq": 2 * to + y_hi}
        )

    def d_copy(t, i):
        src = (dq_out, dk_out, dv_out)[t]
        dst = dqkv_ref.at[0, :, block(t * n + s, LANES)]
        return remote(src.at[i], dst, d_send.at[t, i], d_recv.at[t, i], {"seq": behind(s, i)})

    def each(first, step, last=n):
        def body(i, carry):
            step(i)
            return carry

        lax.fori_loop(first, last, body, 0)

    local = [
        pltpu.make_async_copy(k_ref.at[0, :, block(s, LANES)], k_in.at[0], local_sem.at[0]),
        pltpu.make_async_copy(v_ref.at[0, :, block(s, LANES)], v_in.at[0], local_sem.at[1]),
        pltpu.make_async_copy(q_ref.at[0, :, block(s, LANES)], q_in.at[0], local_sem.at[2]),
        pltpu.make_async_copy(w_ref, w_all.at[0, my_half, :], local_sem.at[3]),
        pltpu.make_async_copy(go_ref.at[0], go, local_sem.at[4]),
    ]
    for copy in local:
        copy.start()

    barrier = pltpu.get_barrier_semaphore()

    def greet(where):
        pl.semaphore_signal(barrier, inc=1, device_id=where, device_id_type=pl.DeviceIdType.MESH)

    each(1, lambda i: greet({"seq": ahead(s, i)}))
    for dx in range(1, X):
        greet(device_at(0, dx))
    greet(device_at(1, 0))
    greet({"seq": 2 * z + 1 - y_hi, **device_at(1, 0)})
    greet(sibling)
    pl.semaphore_wait(barrier, n - 1 + X - 1 + 3)

    for slot in (4, 3, 1):
        w_copy(slot).start()
    for t in (0, 2, 1):
        each(1, lambda i: qkv_copy(t, i).start())
    ws_copy(0).start()
    for copy in local:
        copy.wait()
    for c in range(n):
        cut = slice(c * columns, (c + 1) * columns)
        go_t[cut, :] = go[:, cut].astype(F32).T.astype(BF16)

    def turn(src, dst, i):
        dst[:, block(i, rows)] = src[i].astype(F32).T.astype(BF16)

    def hand_on(slot, *nexts):
        w_copy(slot).wait_recv()
        for following in nexts:
            w_copy(following).start()
        ws_copy(slot).start()

    hand_on(4, 7, 5)
    each(1, lambda i: qkv_copy(0, i).wait_recv())

    k_rows = k_in.reshape(length, LANES)
    v_rows = v_in.reshape(length, LANES)

    def grad_attn(*slots):
        for slot in slots:
            ws_copy(slot).wait_recv()
        both = dot(jnp.concatenate([w_all[slot] for slot in slots], axis=0), go_t[...]).astype(BF16)
        for at, slot in enumerate(slots):
            i = behind(chip_at(slot // X, slot % X), s)
            g = both[at * LANES : (at + 1) * LANES]

            @pl.when(i == 0)
            def _():
                g_in[0] = g

            @pl.when(i > 0)
            def _():
                g_out[i] = g
                g_copy(i).start()

    def weight_part(b):
        first = b * batch
        each(max(first, 1), lambda i: o_copy(i).wait_recv(), first + batch)
        for i in range(batch):
            o_rows[i * half : (i + 1) * half, :] = o_in[first + i, my_half, :]
            o_rows[(batch + i) * half : (batch + i + 1) * half, :] = o_in[first + i, block(1 - core, half), :]
        for c in range(n):
            cut = slice(c * columns, (c + 1) * columns)
            part = dot(o_rows[...], go[:, cut]).astype(BF16)
            own_part[first : first + batch, :, cut] = part[: batch * half].reshape(batch, half, columns)
            sib_out[first : first + batch, :, cut] = part[batch * half :].reshape(batch, half, columns)
        sib_copy(b).start()

    def share(b):
        sib_copy(b).wait_recv()

        def send(i):
            dy, dx = where_to(i)
            pair = own_part[i].astype(F32) + sib_in[i].astype(F32)

            @pl.when(dx == 0)
            def _():
                home[dy] = pair

            @pl.when(dx > 0)
            def _():
                rs_out[i] = pair.astype(BF16)
                rs_copy(i).start()

        each(b * batch, send, (b + 1) * batch)

    def row_sum():
        for slot in range(1, 2 * X):
            if slot != X:
                rs_arrival(slot).wait_recv()
        for c in range(Z):
            cut = slice(c * quarter, (c + 1) * quarter)
            for dy in range(2):
                value = home[dy, :, cut]
                for dx in range(1, X):
                    value += rs_in[dy * X + dx, :, cut].astype(F32)
                total[c, dy] = value
                zs_out[c, dy] = value.astype(BF16)
        for k in range(1, Z):
            zs_copy(k).start()

    def patch_sum():
        for k in range(1, Z):
            zs_copy(k).wait_recv()
        for dy in range(2):
            value = total[z, dy]
            for k in range(1, Z):
                value += zs_in[k, dy].astype(F32)
            ys_out[dy] = value.astype(BF16)
        for k in range(3):
            ys_copy(k).start()
        ys_in[2 * y_hi + y] = ys_out[0]

    def weight_out():
        for k in range(3):
            ys_copy(k).wait_recv()
        value = ys_in[0].astype(F32)
        for at in range(1, 4):
            value += ys_in[at].astype(F32)
        done[...] = value.astype(BF16)
        for k in range(1, Z):
            gw_copy(k).start()
        gw_ref[:, block(z, quarter)] = done[...].astype(F32)

    def column(value):
        return jnp.broadcast_to(value, (8, wide)).T[:, 0:1]

    def scaled_rows(natural, scale):
        lane = lax.broadcasted_iota(jnp.int32, natural.shape, 1)
        first = jnp.where(lane < half, natural * scale[:rows], 0.0)
        second = jnp.where(lane < half, 0.0, natural * scale[rows:])
        return jnp.concatenate([first, second], axis=0).astype(BF16)

    def probs(i, with_out):
        @pl.when(i > 0)
        def _():
            qkv_copy(2, i).wait_recv()

        q = q_in[i].astype(F32)
        q_t[...] = split_heads(q.T).astype(BF16)

        def score_chunk(c, top):
            keys = block(c, CHUNK)
            value = dot(k_rows[keys, :], q_t[...])
            score[keys, :] = value
            return jnp.maximum(top, jnp.max(value.reshape(CHUNK // 8, 8, wide), axis=0))

        top = lax.fori_loop(0, chunks, score_chunk, jnp.full((8, wide), -jnp.inf, F32), unroll=True)
        top = jnp.max(top, axis=0, keepdims=True)
        if with_out:
            out_t[...] = jnp.zeros_like(out_t)

        def prob_chunk(c, norm):
            keys = block(c, CHUNK)
            p = jnp.exp2((score[keys, :] - top) * EXP_SCALE)
            low = p.astype(BF16)
            prob[keys, block(i, wide)] = low
            if with_out:
                out_t[...] += dot(v_t[:, keys], low)
            return norm + jnp.sum(p.reshape(CHUNK // 8, 8, wide), axis=0)

        norm = lax.fori_loop(0, chunks, prob_chunk, jnp.zeros((8, wide), F32), unroll=True)
        inverse = 1.0 / jnp.sum(norm, axis=0, keepdims=True)
        inv_sum[i] = jnp.broadcast_to(inverse, (8, wide))
        q_l[block(i, wide), :] = scaled_rows(q, column(inverse * SCALING))
        if with_out:
            send_out(i, out_t[...] * inverse)

    def send_out(i, wide_out):
        merged = merge_heads(wide_out)
        out_all[i] = merged

        @pl.when(i == 0)
        def _():
            o_in[0] = merged.astype(BF16)

        @pl.when(i > 0)
        def _():
            o_out[i] = merged.astype(BF16)
            o_copy(i).start()

    def early(i, carry):
        probs(i, False)

        @pl.when(i == 0)
        def _():
            hand_on(3, 2)
            hand_on(1)
            grad_attn(0, 4)

        @pl.when(i == 1)
        def _():
            hand_on(5, 6)
            grad_attn(3, 1)

        @pl.when(i == 2)
        def _():
            hand_on(7)

        return carry

    def late(i, carry):
        probs(i, True)

        @pl.when(i == EARLY)
        def _():
            grad_attn(2, 6)

        @pl.when(i == batch + 1)
        def _():
            weight_part(0)

        @pl.when(i == batch + 2)
        def _():
            share(0)

        return carry

    lax.fori_loop(0, EARLY, early, 0)
    turn(k_in, k_t, 0)
    each(1, lambda i: turn(k_in, k_t, i))
    grad_attn(5, 7)
    turn(v_in, v_t, 0)

    def arrive(i):
        qkv_copy(1, i).wait_recv()
        turn(v_in, v_t, i)

    each(1, arrive)
    each(0, lambda i: send_out(i, dot(v_t[...], prob[:, block(i, wide)]) * inv_sum[i, 0:1, :]), EARLY)
    hand_on(2)
    hand_on(6)
    lax.fori_loop(EARLY, n, late, 0)

    def prepare(i, carry):
        @pl.when(i > 0)
        def _():
            g_copy(i).wait_recv()

        g = g_in[i].astype(F32)
        g_t[:, block(i, wide)] = split_heads(g).astype(BF16)
        g_l[block(i, wide), :] = scaled_rows(g.T, column(inv_sum[i, 0:1, :]))
        product = out_all[i] * g
        both = jnp.concatenate(
            [
                jnp.sum(product[:half], axis=0, keepdims=True),
                jnp.sum(product[half:], axis=0, keepdims=True),
            ],
            axis=1,
        )
        row_dot[i] = jnp.broadcast_to(both, (8, wide))
        return carry

    lax.fori_loop(0, n, prepare, 0)
    weight_part(1)
    dq_t[...] = jnp.zeros_like(dq_t)
    share(1)

    def grad_q(i):
        return merge_heads(dq_t[:, block(i, wide)] * (inv_sum[i, 0:1, :] * SCALING)).T.astype(BF16)

    def backward(j, last):
        keys = block(j, span)

        def grad_chunk(i):
            cut = block(i, wide)
            grad_prob = dot(v_rows[keys, :], g_t[:, cut])
            grad_score = (prob[keys, cut].astype(F32) * (grad_prob - row_dot[i, 0:1, :])).astype(BF16)
            ds_buf[:, cut] = grad_score
            dq_t[:, cut] += dot(k_t[:, keys], grad_score)
            if last:
                dq_out[i] = grad_q(i)
                if i:
                    d_copy(0, i).start()

        for i in range(n):
            grad_chunk(i)
        grad_v = dot(prob[keys, :], g_l[...]).astype(BF16)
        grad_k = dot(ds_buf[...], q_l[...]).astype(BF16)

        for part in range(SPAN):
            i = j * SPAN + part
            cut = slice(part * rows, (part + 1) * rows)
            dk_out[i] = grad_k[cut]
            dv_out[i] = grad_v[cut]

            @pl.when(i > 0)
            def _():
                d_copy(1, i).start()
                d_copy(2, i).start()

    def backward_step(j, carry):
        backward(j, False)

        @pl.when(j == steps - 3)
        def _():
            row_sum()

        @pl.when(j == steps - 2)
        def _():
            patch_sum()

        return carry

    lax.fori_loop(0, steps - 1, backward_step, 0)
    backward(steps - 1, True)
    weight_out()
    for t in range(3):
        dqkv_ref[0, :, block(t * n + s, LANES)] = (dq_out, dk_out, dv_out)[t][0]

    def arrivals(i):
        for t in range(3):
            d_copy(t, i).wait_recv()

    each(1, arrivals)

    def sent(i):
        for t in range(3):
            qkv_copy(t, i).wait_send()
            d_copy(t, i).wait_send()
        g_copy(i).wait_send()
        o_copy(i).wait_send()

    each(1, sent)
    for slot in range(n):
        if slot:
            w_copy(slot).wait_send()
        ws_copy(slot).wait_send()
    sib_copy(0).wait_send()
    sib_copy(1).wait_send()
    for k in range(3):
        ys_copy(k).wait_send()
        zs_copy(k + 1).wait_send()
        gw_copy(k + 1).wait_send()
        gw_copy(k + 1).wait_recv()
        gw_ref[:, block(lax.rem(z + Z - k - 1, Z), quarter)] = gw_in[k + 1].astype(F32)

    def rs_sent(i):
        @pl.when(where_to(i)[1] > 0)
        def _():
            rs_copy(i).wait_send()

    each(0, rs_sent)


def on_device(n, queries, keys, values, out_proj, grad_out):
    rows, features = queries.shape[1:]
    share_rows, width = out_proj.shape
    length = n * rows
    wide = 2 * rows
    columns = width // n
    vmem = pltpu.VMEM
    dma = pltpu.SemaphoreType.DMA
    flat = vmem((n, rows, LANES), BF16)
    turned = vmem((n, LANES, rows), BF16)
    shares = vmem((n, HEAD_DIM, width), BF16)
    return pl.pallas_call(
        functools.partial(kernel, n, rows, width),
        out_shape=(
            vmem((1, rows, 3 * features), BF16),
            vmem((share_rows, width), F32),
        ),
        in_specs=[pl.BlockSpec(memory_space=pl.ANY)] * 5,
        out_specs=[pl.BlockSpec(memory_space=vmem)] * 2,
        scratch_shapes=[
            flat, flat, flat, turned,
            vmem((n, LANES, width), BF16),
            vmem((rows, width), BF16),
            vmem((width, rows), BF16),
            vmem((LANES, length), BF16),
            vmem((LANES, length), BF16),
            vmem((length, wide), F32),
            vmem((length, n * wide), BF16),
            vmem((LANES, wide), BF16),
            vmem((LANES, wide), F32),
            vmem((n, 8, wide), F32),
            vmem((n, LANES, rows), F32),
            vmem((n, 8, wide), F32),
            vmem((LANES, n * wide), BF16),
            vmem((n * wide, LANES), BF16),
            vmem((n * wide, LANES), BF16),
            vmem((SPAN * rows, n * wide), BF16),
            vmem((LANES, n * wide), F32),
            turned, turned, turned,
            vmem((n * HEAD_DIM, rows), BF16),
            shares, shares, shares, shares, shares,
            vmem((2, HEAD_DIM, width), F32),
            vmem((Z, 2, HEAD_DIM, width // Z), F32),
            vmem((Z, 2, HEAD_DIM, width // Z), BF16),
            vmem((Z, 2, HEAD_DIM, width // Z), BF16),
            vmem((2, HEAD_DIM, width // Z), BF16),
            vmem((4, HEAD_DIM, width // Z), BF16),
            vmem((HEAD_DIM, width // Z), BF16),
            vmem((Z, HEAD_DIM, width // Z), BF16),
            flat, flat, flat,
            dma((3, n)), dma((3, n)),
            dma((n,)), dma((n,)), dma((n,)), dma((n,)),
            dma((n,)), dma((n,)), dma((n,)), dma((n,)),
            dma((2,)), dma((2,)), dma((n,)), dma((n,)),
            dma((Z,)), dma((Z,)), dma((3,)), dma((3,)), dma((Z,)), dma((Z,)),
            dma((3, n)), dma((3, n)), dma((5,)),
        ],
        compiler_params=pltpu.CompilerParams(
            collective_id=0, has_side_effects=True, vmem_limit_bytes=60 << 20
        ),
    )(queries, keys, values, out_proj, grad_out)


def solution(mesh):
    return jax.shard_map(
        functools.partial(on_device, mesh.shape["seq"]),
        mesh=mesh,
        in_specs=(
            P("dp", "seq", None),
            P("dp", "seq", None),
            P("dp", "seq", None),
            P("dp", None),
            P("dp", "seq", None),
        ),
        out_specs=(P("dp", "seq", None), P("dp", None)),
        check_vma=False,
    )
```

```python
import functools
import math

import jax
import jax.numpy as jnp
from jax import lax
from jax.experimental import pallas as pl
from jax.experimental.pallas import tpu as pltpu
from jax.sharding import PartitionSpec as P

HEAD_DIM = 64
LANES = 2 * HEAD_DIM
X = 4
Z = 4
SPAN = 2
EARLY = 2
CHUNK = 512
SCALING = HEAD_DIM ** (-0.5)
EXP_SCALE = SCALING * math.log2(math.e)
F32 = jnp.float32
BF16 = jnp.bfloat16


def dot(a, b):
    return jnp.dot(a, b, preferred_element_type=F32)


def dot_nt(a, b):
    return lax.dot_general(a, b, (((1,), (1,)), ((), ())), preferred_element_type=F32)


def split_heads(columns):
    row = lax.broadcasted_iota(jnp.int32, columns.shape, 0)
    zeros = jnp.zeros_like(columns)
    return jnp.concatenate(
        [jnp.where(row < HEAD_DIM, columns, zeros), jnp.where(row < HEAD_DIM, zeros, columns)], axis=1
    )


def merge_heads(wide):
    rows = wide.shape[1] // 2
    first, second = wide[:, :rows], wide[:, rows:]
    row = lax.broadcasted_iota(jnp.int32, first.shape, 0)
    return jnp.where(row < HEAD_DIM, first, second)


def kernel(
    n, rows, width,
    q_ref, k_ref, v_ref, w_ref, go_ref, dqkv_ref, gw_ref,
    q_in, k_in, v_in, g_in, w_all, go, go_t, k_t, v_t,
    score, prob, q_t, out_t, inv_sum, out_all, row_dot, g_t, g_l, q_l, ds_buf, dq_t,
    g_out, o_out, o_in, o_rows, own_part, sib_out, sib_in, rs_out, rs_in, home,
    total, zs_out, zs_in, ys_out, ys_in, done, gw_in, dq_out, dk_out, dv_out,
    qkv_send, qkv_recv, w_send, w_recv, ws_send, ws_recv, g_send, g_recv, o_send, o_recv,
    sib_send, sib_recv, rs_send, rs_recv, zs_send, zs_recv, ys_send, ys_recv, gw_send, gw_recv,
    d_send, d_recv, local_sem,
):
    s = lax.axis_index("seq")
    d = lax.axis_index("dp")
    chip, core = d // 2, lax.rem(d, 2)
    y, x = chip // X, lax.rem(chip, X)
    z, y_hi = s // 2, lax.rem(s, 2)
    quarter = width // Z
    length = n * rows
    chunks = length // CHUNK
    wide = 2 * rows
    half = HEAD_DIM
    columns = width // n
    batch = n // 2
    span = SPAN * rows
    steps = n // SPAN

    def ahead(base, i):
        return lax.rem(base + i, n)

    def behind(base, i):
        return lax.rem(base + n - i, n)

    def block(index, size):
        return pl.ds(pl.multiple_of(index * size, size), size)

    def remote(src, dst, send, recv, where):
        return pltpu.make_async_remote_copy(
            src_ref=src, dst_ref=dst, send_sem=send, recv_sem=recv,
            device_id=where, device_id_type=pl.DeviceIdType.MESH,
        )

    my_half = block(core, half)
    sibling = {"dp": 2 * chip + 1 - core}

    def chip_at(dy, dx):
        return lax.rem(y + dy, 2) * X + lax.rem(x + dx, X)

    def device_at(dy, dx):
        return {"dp": 2 * chip_at(dy, dx) + core}

    def qkv_copy(t, i):
        src, dst = ((k_ref, k_in), (v_ref, v_in), (q_ref, q_in))[t]
        peer = ahead(s, i)
        return remote(
            src.at[0, :, block(peer, LANES)], dst.at[i], qkv_send.at[t, i], qkv_recv.at[t, i], {"seq": peer}
        )

    def w_copy(slot):
        src = {7: 4, 5: 4, 2: 3, 6: 5}.get(slot)
        dy, dx = {3: (0, 1), 1: (0, 3), 4: (1, 0), 7: (0, 1), 5: (0, 3), 2: (0, 1), 6: (0, 3)}[slot]
        return remote(
            w_ref if src is None else w_all.at[src, my_half, :],
            w_all.at[slot, my_half, :], w_send.at[slot], w_recv.at[slot], device_at(dy, dx),
        )

    def ws_copy(slot):
        part = w_all.at[slot, my_half, :]
        return remote(w_ref if slot == 0 else part, part, ws_send.at[slot], ws_recv.at[slot], sibling)

    def g_copy(i):
        return remote(g_out.at[i], g_in.at[i], g_send.at[i], g_recv.at[i], {"seq": ahead(s, i)})

    def o_copy(i):
        return remote(o_out.at[i], o_in.at[i], o_send.at[i], o_recv.at[i], {"seq": behind(s, i)})

    def sib_copy(b):
        part = pl.ds(b * batch, batch)
        return remote(sib_out.at[part], sib_in.at[part], sib_send.at[b], sib_recv.at[b], sibling)

    def where_to(i):
        h = ahead(s, i)
        return lax.rem(h // X + y, 2), lax.rem(lax.rem(h, X) + X - x, X)

    def rs_copy(i):
        dy, dx = where_to(i)
        slot = dy * X + lax.rem(X - dx, X)
        return remote(rs_out.at[i], rs_in.at[slot], rs_send.at[i], rs_recv.at[slot], device_at(0, dx))

    def rs_arrival(slot):
        return remote(rs_out.at[0], rs_in.at[slot], rs_send.at[0], rs_recv.at[slot], device_at(0, 1))

    def zs_copy(k):
        to = lax.rem(z + k, Z)
        return remote(
            zs_out.at[to], zs_in.at[k], zs_send.at[k], zs_recv.at[k], {"seq": 2 * to + y_hi}
        )

    def ys_copy(k):
        dy, dh = ((1, 0), (1, 1), (0, 1))[k]
        where = {
            "seq": 2 * z + lax.rem(y_hi + dh, 2),
            "dp": 2 * chip_at(dy, 0) + core,
        }
        return remote(ys_out.at[dy], ys_in.at[2 * y_hi + y], ys_send.at[k], ys_recv.at[k], where)

    def gw_copy(k):
        to = lax.rem(z + k, Z)
        return remote(
            done, gw_in.at[k], gw_send.at[k], gw_recv.at[k], {"seq": 2 * to + y_hi}
        )

    def d_copy(t, i):
        src = (dq_out, dk_out, dv_out)[t]
        dst = dqkv_ref.at[0, :, block(t * n + s, LANES)]
        return remote(src.at[i], dst, d_send.at[t, i], d_recv.at[t, i], {"seq": behind(s, i)})

    def each(first, step, last=n):
        def body(i, carry):
            step(i)
            return carry

        lax.fori_loop(first, last, body, 0)

    local = [
        pltpu.make_async_copy(k_ref.at[0, :, block(s, LANES)], k_in.at[0], local_sem.at[0]),
        pltpu.make_async_copy(v_ref.at[0, :, block(s, LANES)], v_in.at[0], local_sem.at[1]),
        pltpu.make_async_copy(q_ref.at[0, :, block(s, LANES)], q_in.at[0], local_sem.at[2]),
        pltpu.make_async_copy(w_ref, w_all.at[0, my_half, :], local_sem.at[3]),
        pltpu.make_async_copy(go_ref.at[0], go, local_sem.at[4]),
    ]
    for copy in local:
        copy.start()

    barrier = pltpu.get_barrier_semaphore()

    def greet(where):
        pl.semaphore_signal(barrier, inc=1, device_id=where, device_id_type=pl.DeviceIdType.MESH)

    each(1, lambda i: greet({"seq": ahead(s, i)}))
    for dx in range(1, X):
        greet(device_at(0, dx))
    greet(device_at(1, 0))
    greet({"seq": 2 * z + 1 - y_hi, **device_at(1, 0)})
    greet(sibling)
    pl.semaphore_wait(barrier, n - 1 + X - 1 + 3)

    for slot in (4, 3, 1):
        w_copy(slot).start()
    for t in (0, 2, 1):
        each(1, lambda i: qkv_copy(t, i).start())
    ws_copy(0).start()
    for copy in local:
        copy.wait()
    for c in range(n):
        cut = slice(c * columns, (c + 1) * columns)
        go_t[cut, :] = go[:, cut].astype(F32).T.astype(BF16)

    def turn(src, dst, i):
        dst[:, block(i, rows)] = src[i].astype(F32).T.astype(BF16)

    def hand_on(slot, *nexts):
        w_copy(slot).wait_recv()
        for following in nexts:
            w_copy(following).start()
        ws_copy(slot).start()

    hand_on(4, 7, 5)
    each(1, lambda i: qkv_copy(0, i).wait_recv())

    k_rows = k_in.reshape(length, LANES)
    v_rows = v_in.reshape(length, LANES)

    def grad_attn(*slots):
        for slot in slots:
            ws_copy(slot).wait_recv()
        both = dot(jnp.concatenate([w_all[slot] for slot in slots], axis=0), go_t[...]).astype(BF16)
        for at, slot in enumerate(slots):
            i = behind(chip_at(slot // X, slot % X), s)
            g = both[at * LANES : (at + 1) * LANES]

            @pl.when(i == 0)
            def _():
                g_in[0] = g

            @pl.when(i > 0)
            def _():
                g_out[i] = g
                g_copy(i).start()

    def weight_part(b):
        first = b * batch
        each(max(first, 1), lambda i: o_copy(i).wait_recv(), first + batch)
        for i in range(batch):
            o_rows[i * half : (i + 1) * half, :] = o_in[first + i, my_half, :]
            o_rows[(batch + i) * half : (batch + i + 1) * half, :] = o_in[first + i, block(1 - core, half), :]
        for c in range(n):
            cut = slice(c * columns, (c + 1) * columns)
            part = dot(o_rows[...], go[:, cut]).astype(BF16)
            own_part[first : first + batch, :, cut] = part[: batch * half].reshape(batch, half, columns)
            sib_out[first : first + batch, :, cut] = part[batch * half :].reshape(batch, half, columns)
        sib_copy(b).start()

    def share(b):
        sib_copy(b).wait_recv()

        def send(i):
            dy, dx = where_to(i)
            pair = own_part[i].astype(F32) + sib_in[i].astype(F32)

            @pl.when(dx == 0)
            def _():
                home[dy] = pair

            @pl.when(dx > 0)
            def _():
                rs_out[i] = pair.astype(BF16)
                rs_copy(i).start()

        each(b * batch, send, (b + 1) * batch)

    def row_sum():
        for slot in range(1, 2 * X):
            if slot != X:
                rs_arrival(slot).wait_recv()
        for c in range(Z):
            cut = slice(c * quarter, (c + 1) * quarter)
            for dy in range(2):
                value = home[dy, :, cut]
                for dx in range(1, X):
                    value += rs_in[dy * X + dx, :, cut].astype(F32)
                total[c, dy] = value
                zs_out[c, dy] = value.astype(BF16)
        for k in range(1, Z):
            zs_copy(k).start()

    def patch_sum():
        for k in range(1, Z):
            zs_copy(k).wait_recv()
        for dy in range(2):
            value = total[z, dy]
            for k in range(1, Z):
                value += zs_in[k, dy].astype(F32)
            ys_out[dy] = value.astype(BF16)
        for k in range(3):
            ys_copy(k).start()
        ys_in[2 * y_hi + y] = ys_out[0]

    def weight_out():
        for k in range(3):
            ys_copy(k).wait_recv()
        value = ys_in[0].astype(F32)
        for at in range(1, 4):
            value += ys_in[at].astype(F32)
        done[...] = value.astype(BF16)
        for k in range(1, Z):
            gw_copy(k).start()
        gw_ref[:, block(z, quarter)] = done[...].astype(F32)

    def column(value):
        return jnp.broadcast_to(value, (8, wide)).T[:, 0:1]

    def scaled_rows(natural, scale):
        lane = lax.broadcasted_iota(jnp.int32, natural.shape, 1)
        first = jnp.where(lane < half, natural * scale[:rows], 0.0)
        second = jnp.where(lane < half, 0.0, natural * scale[rows:])
        return jnp.concatenate([first, second], axis=0).astype(BF16)

    def probs(i, with_out):
        @pl.when(i > 0)
        def _():
            qkv_copy(2, i).wait_recv()

        q = q_in[i].astype(F32)
        q_t[...] = split_heads(q.T).astype(BF16)

        def score_chunk(c, top):
            keys = block(c, CHUNK)
            value = dot(k_rows[keys, :], q_t[...])
            score[keys, :] = value
            return jnp.maximum(top, jnp.max(value.reshape(CHUNK // 8, 8, wide), axis=0))

        top = lax.fori_loop(0, chunks, score_chunk, jnp.full((8, wide), -jnp.inf, F32), unroll=True)
        top = jnp.max(top, axis=0, keepdims=True)
        if with_out:
            out_t[...] = jnp.zeros_like(out_t)

        def prob_chunk(c, norm):
            keys = block(c, CHUNK)
            p = jnp.exp2((score[keys, :] - top) * EXP_SCALE)
            low = p.astype(BF16)
            prob[keys, block(i, wide)] = low
            if with_out:
                out_t[...] += dot(v_t[:, keys], low)
            return norm + jnp.sum(p.reshape(CHUNK // 8, 8, wide), axis=0)

        norm = lax.fori_loop(0, chunks, prob_chunk, jnp.zeros((8, wide), F32), unroll=True)
        inverse = 1.0 / jnp.sum(norm, axis=0, keepdims=True)
        inv_sum[i] = jnp.broadcast_to(inverse, (8, wide))
        q_l[block(i, wide), :] = scaled_rows(q, column(inverse * SCALING))
        if with_out:
            send_out(i, out_t[...] * inverse)

    def send_out(i, wide_out):
        merged = merge_heads(wide_out)
        out_all[i] = merged

        @pl.when(i == 0)
        def _():
            o_in[0] = merged.astype(BF16)

        @pl.when(i > 0)
        def _():
            o_out[i] = merged.astype(BF16)
            o_copy(i).start()

    def early(i, carry):
        probs(i, False)

        @pl.when(i == 0)
        def _():
            hand_on(3, 2)
            hand_on(1)
            grad_attn(0, 4)

        @pl.when(i == 1)
        def _():
            hand_on(5, 6)
            grad_attn(3, 1)

        return carry

    def late(i, carry):
        probs(i, True)

        @pl.when(i == EARLY)
        def _():
            grad_attn(2, 6)

        @pl.when(i == batch + 2)
        def _():
            weight_part(0)

        @pl.when(i == batch + 3)
        def _():
            share(0)

        return carry

    lax.fori_loop(0, EARLY, early, 0)
    hand_on(7)
    turn(k_in, k_t, 0)
    each(1, lambda i: turn(k_in, k_t, i))
    grad_attn(5, 7)
    turn(v_in, v_t, 0)

    def arrive(i):
        qkv_copy(1, i).wait_recv()
        turn(v_in, v_t, i)

    each(1, arrive)
    each(0, lambda i: send_out(i, dot(v_t[...], prob[:, block(i, wide)]) * inv_sum[i, 0:1, :]), EARLY)
    hand_on(2)
    hand_on(6)
    lax.fori_loop(EARLY, n, late, 0)

    def prepare(i, carry):
        @pl.when(i > 0)
        def _():
            g_copy(i).wait_recv()

        g = g_in[i].astype(F32)
        g_t[:, block(i, wide)] = split_heads(g).astype(BF16)
        g_l[block(i, wide), :] = scaled_rows(g.T, column(inv_sum[i, 0:1, :]))
        product = out_all[i] * g
        both = jnp.concatenate(
            [
                jnp.sum(product[:half], axis=0, keepdims=True),
                jnp.sum(product[half:], axis=0, keepdims=True),
            ],
            axis=1,
        )
        row_dot[i] = jnp.broadcast_to(both, (8, wide))
        return carry

    lax.fori_loop(0, n, prepare, 0)
    weight_part(1)
    dq_t[...] = jnp.zeros_like(dq_t)
    share(1)

    def grad_q(i):
        return merge_heads(dq_t[:, block(i, wide)] * (inv_sum[i, 0:1, :] * SCALING)).T.astype(BF16)

    def backward(j, last):
        keys = block(j, span)

        def grad_chunk(i):
            cut = block(i, wide)
            grad_prob = dot(v_rows[keys, :], g_t[:, cut])
            grad_score = (prob[keys, cut].astype(F32) * (grad_prob - row_dot[i, 0:1, :])).astype(BF16)
            ds_buf[:, cut] = grad_score
            dq_t[:, cut] += dot(k_t[:, keys], grad_score)
            if last:
                dq_out[i] = grad_q(i)
                if i:
                    d_copy(0, i).start()

        for i in range(n):
            grad_chunk(i)
        grad_v = dot(prob[keys, :], g_l[...]).astype(BF16)
        grad_k = dot(ds_buf[...], q_l[...]).astype(BF16)

        for part in range(SPAN):
            i = j * SPAN + part
            cut = slice(part * rows, (part + 1) * rows)
            dk_out[i] = grad_k[cut]
            dv_out[i] = grad_v[cut]

            @pl.when(i > 0)
            def _():
                d_copy(1, i).start()
                d_copy(2, i).start()

    def backward_step(j, carry):
        backward(j, False)

        @pl.when(j == steps - 3)
        def _():
            row_sum()

        @pl.when(j == steps - 2)
        def _():
            patch_sum()

        return carry

    lax.fori_loop(0, steps - 1, backward_step, 0)
    backward(steps - 1, True)
    weight_out()
    for t in range(3):
        dqkv_ref[0, :, block(t * n + s, LANES)] = (dq_out, dk_out, dv_out)[t][0]

    def arrivals(i):
        for t in range(3):
            d_copy(t, i).wait_recv()

    each(1, arrivals)

    def sent(i):
        for t in range(3):
            qkv_copy(t, i).wait_send()
            d_copy(t, i).wait_send()
        g_copy(i).wait_send()
        o_copy(i).wait_send()

    each(1, sent)
    for slot in range(n):
        if slot:
            w_copy(slot).wait_send()
        ws_copy(slot).wait_send()
    sib_copy(0).wait_send()
    sib_copy(1).wait_send()
    for k in range(3):
        ys_copy(k).wait_send()
        zs_copy(k + 1).wait_send()
        gw_copy(k + 1).wait_send()
        gw_copy(k + 1).wait_recv()
        gw_ref[:, block(lax.rem(z + Z - k - 1, Z), quarter)] = gw_in[k + 1].astype(F32)

    def rs_sent(i):
        @pl.when(where_to(i)[1] > 0)
        def _():
            rs_copy(i).wait_send()

    each(0, rs_sent)


def on_device(n, queries, keys, values, out_proj, grad_out):
    rows, features = queries.shape[1:]
    share_rows, width = out_proj.shape
    length = n * rows
    wide = 2 * rows
    columns = width // n
    vmem = pltpu.VMEM
    dma = pltpu.SemaphoreType.DMA
    flat = vmem((n, rows, LANES), BF16)
    turned = vmem((n, LANES, rows), BF16)
    shares = vmem((n, HEAD_DIM, width), BF16)
    return pl.pallas_call(
        functools.partial(kernel, n, rows, width),
        out_shape=(
            vmem((1, rows, 3 * features), BF16),
            vmem((share_rows, width), F32),
        ),
        in_specs=[pl.BlockSpec(memory_space=pl.ANY)] * 5,
        out_specs=[pl.BlockSpec(memory_space=vmem)] * 2,
        scratch_shapes=[
            flat, flat, flat, turned,
            vmem((n, LANES, width), BF16),
            vmem((rows, width), BF16),
            vmem((width, rows), BF16),
            vmem((LANES, length), BF16),
            vmem((LANES, length), BF16),
            vmem((length, wide), F32),
            vmem((length, n * wide), BF16),
            vmem((LANES, wide), BF16),
            vmem((LANES, wide), F32),
            vmem((n, 8, wide), F32),
            vmem((n, LANES, rows), F32),
            vmem((n, 8, wide), F32),
            vmem((LANES, n * wide), BF16),
            vmem((n * wide, LANES), BF16),
            vmem((n * wide, LANES), BF16),
            vmem((SPAN * rows, n * wide), BF16),
            vmem((LANES, n * wide), F32),
            turned, turned, turned,
            vmem((n * HEAD_DIM, rows), BF16),
            shares, shares, shares, shares, shares,
            vmem((2, HEAD_DIM, width), F32),
            vmem((Z, 2, HEAD_DIM, width // Z), F32),
            vmem((Z, 2, HEAD_DIM, width // Z), BF16),
            vmem((Z, 2, HEAD_DIM, width // Z), BF16),
            vmem((2, HEAD_DIM, width // Z), BF16),
            vmem((4, HEAD_DIM, width // Z), BF16),
            vmem((HEAD_DIM, width // Z), BF16),
            vmem((Z, HEAD_DIM, width // Z), BF16),
            flat, flat, flat,
            dma((3, n)), dma((3, n)),
            dma((n,)), dma((n,)), dma((n,)), dma((n,)),
            dma((n,)), dma((n,)), dma((n,)), dma((n,)),
            dma((2,)), dma((2,)), dma((n,)), dma((n,)),
            dma((Z,)), dma((Z,)), dma((3,)), dma((3,)), dma((Z,)), dma((Z,)),
            dma((3, n)), dma((3, n)), dma((5,)),
        ],
        compiler_params=pltpu.CompilerParams(
            collective_id=0, has_side_effects=True, vmem_limit_bytes=60 << 20
        ),
    )(queries, keys, values, out_proj, grad_out)


def solution(mesh):
    return jax.shard_map(
        functools.partial(on_device, mesh.shape["seq"]),
        mesh=mesh,
        in_specs=(
            P("dp", "seq", None),
            P("dp", "seq", None),
            P("dp", "seq", None),
            P("dp", None),
            P("dp", "seq", None),
        ),
        out_specs=(P("dp", "seq", None), P("dp", None)),
        check_vma=False,
    )
```

```python
import functools
import math

import jax
import jax.numpy as jnp
from jax import lax
from jax.experimental import pallas as pl
from jax.experimental.pallas import tpu as pltpu
from jax.sharding import PartitionSpec as P

HEAD_DIM = 64
LANES = 2 * HEAD_DIM
X = 4
Z = 4
SPAN = 2
EARLY = 2
CHUNK = 512
SCALING = HEAD_DIM ** (-0.5)
EXP_SCALE = SCALING * math.log2(math.e)
F32 = jnp.float32
BF16 = jnp.bfloat16


def dot(a, b):
    return jnp.dot(a, b, preferred_element_type=F32)


def dot_nt(a, b):
    return lax.dot_general(a, b, (((1,), (1,)), ((), ())), preferred_element_type=F32)


def split_heads(columns):
    row = lax.broadcasted_iota(jnp.int32, columns.shape, 0)
    zeros = jnp.zeros_like(columns)
    return jnp.concatenate(
        [jnp.where(row < HEAD_DIM, columns, zeros), jnp.where(row < HEAD_DIM, zeros, columns)], axis=1
    )


def merge_heads(wide):
    rows = wide.shape[1] // 2
    first, second = wide[:, :rows], wide[:, rows:]
    row = lax.broadcasted_iota(jnp.int32, first.shape, 0)
    return jnp.where(row < HEAD_DIM, first, second)


def kernel(
    n, rows, width,
    q_ref, k_ref, v_ref, w_ref, go_ref, dqkv_ref, gw_ref,
    q_in, k_in, v_in, g_in, w_all, go, go_t, k_t, v_t,
    score, prob, q_t, out_t, inv_sum, out_all, row_dot, g_t, g_l, q_l, ds_buf, dq_t,
    g_out, o_out, o_in, o_rows, own_part, sib_out, sib_in, rs_out, rs_in, home,
    total, zs_out, zs_in, ys_out, ys_in, done, gw_in, dq_out, dk_out, dv_out,
    qkv_send, qkv_recv, w_send, w_recv, ws_send, ws_recv, g_send, g_recv, o_send, o_recv,
    sib_send, sib_recv, rs_send, rs_recv, zs_send, zs_recv, ys_send, ys_recv, gw_send, gw_recv,
    d_send, d_recv, local_sem,
):
    s = lax.axis_index("seq")
    d = lax.axis_index("dp")
    chip, core = d // 2, lax.rem(d, 2)
    y, x = chip // X, lax.rem(chip, X)
    z, y_hi = s // 2, lax.rem(s, 2)
    quarter = width // Z
    length = n * rows
    chunks = length // CHUNK
    wide = 2 * rows
    half = HEAD_DIM
    columns = width // n
    batch = n // 2
    span = SPAN * rows
    steps = n // SPAN

    def ahead(base, i):
        return lax.rem(base + i, n)

    def behind(base, i):
        return lax.rem(base + n - i, n)

    def block(index, size):
        return pl.ds(pl.multiple_of(index * size, size), size)

    def remote(src, dst, send, recv, where):
        return pltpu.make_async_remote_copy(
            src_ref=src, dst_ref=dst, send_sem=send, recv_sem=recv,
            device_id=where, device_id_type=pl.DeviceIdType.MESH,
        )

    my_half = block(core, half)
    sibling = {"dp": 2 * chip + 1 - core}

    def chip_at(dy, dx):
        return lax.rem(y + dy, 2) * X + lax.rem(x + dx, X)

    def device_at(dy, dx):
        return {"dp": 2 * chip_at(dy, dx) + core}

    def qkv_copy(t, i):
        src, dst = ((k_ref, k_in), (v_ref, v_in), (q_ref, q_in))[t]
        peer = ahead(s, i)
        return remote(
            src.at[0, :, block(peer, LANES)], dst.at[i], qkv_send.at[t, i], qkv_recv.at[t, i], {"seq": peer}
        )

    def w_copy(slot):
        src = {7: 4, 5: 4, 2: 3, 6: 5}.get(slot)
        dy, dx = {3: (0, 1), 1: (0, 3), 4: (1, 0), 7: (0, 1), 5: (0, 3), 2: (0, 1), 6: (0, 3)}[slot]
        return remote(
            w_ref if src is None else w_all.at[src, my_half, :],
            w_all.at[slot, my_half, :], w_send.at[slot], w_recv.at[slot], device_at(dy, dx),
        )

    def ws_copy(slot):
        part = w_all.at[slot, my_half, :]
        return remote(w_ref if slot == 0 else part, part, ws_send.at[slot], ws_recv.at[slot], sibling)

    def g_copy(i):
        return remote(g_out.at[i], g_in.at[i], g_send.at[i], g_recv.at[i], {"seq": ahead(s, i)})

    def o_copy(i):
        return remote(o_out.at[i], o_in.at[i], o_send.at[i], o_recv.at[i], {"seq": behind(s, i)})

    def sib_copy(b):
        part = pl.ds(b * batch, batch)
        return remote(sib_out.at[part], sib_in.at[part], sib_send.at[b], sib_recv.at[b], sibling)

    def where_to(i):
        h = ahead(s, i)
        return lax.rem(h // X + y, 2), lax.rem(lax.rem(h, X) + X - x, X)

    def rs_copy(i):
        dy, dx = where_to(i)
        slot = dy * X + lax.rem(X - dx, X)
        return remote(rs_out.at[i], rs_in.at[slot], rs_send.at[i], rs_recv.at[slot], device_at(0, dx))

    def rs_arrival(slot):
        return remote(rs_out.at[0], rs_in.at[slot], rs_send.at[0], rs_recv.at[slot], device_at(0, 1))

    def zs_copy(k):
        to = lax.rem(z + k, Z)
        return remote(
            zs_out.at[to], zs_in.at[k], zs_send.at[k], zs_recv.at[k], {"seq": 2 * to + y_hi}
        )

    def ys_copy(k):
        dy, dh = ((1, 0), (1, 1), (0, 1))[k]
        where = {
            "seq": 2 * z + lax.rem(y_hi + dh, 2),
            "dp": 2 * chip_at(dy, 0) + core,
        }
        return remote(ys_out.at[dy], ys_in.at[2 * y_hi + y], ys_send.at[k], ys_recv.at[k], where)

    def gw_copy(k):
        to = lax.rem(z + k, Z)
        return remote(
            done, gw_in.at[k], gw_send.at[k], gw_recv.at[k], {"seq": 2 * to + y_hi}
        )

    def d_copy(t, i):
        src = (dq_out, dk_out, dv_out)[t]
        dst = dqkv_ref.at[0, :, block(t * n + s, LANES)]
        return remote(src.at[i], dst, d_send.at[t, i], d_recv.at[t, i], {"seq": behind(s, i)})

    def each(first, step, last=n):
        def body(i, carry):
            step(i)
            return carry

        lax.fori_loop(first, last, body, 0)

    local = [
        pltpu.make_async_copy(k_ref.at[0, :, block(s, LANES)], k_in.at[0], local_sem.at[0]),
        pltpu.make_async_copy(v_ref.at[0, :, block(s, LANES)], v_in.at[0], local_sem.at[1]),
        pltpu.make_async_copy(q_ref.at[0, :, block(s, LANES)], q_in.at[0], local_sem.at[2]),
        pltpu.make_async_copy(w_ref, w_all.at[0, my_half, :], local_sem.at[3]),
        pltpu.make_async_copy(go_ref.at[0], go, local_sem.at[4]),
    ]
    for copy in local:
        copy.start()

    barrier = pltpu.get_barrier_semaphore()

    def greet(where):
        pl.semaphore_signal(barrier, inc=1, device_id=where, device_id_type=pl.DeviceIdType.MESH)

    each(1, lambda i: greet({"seq": ahead(s, i)}))
    for dx in range(1, X):
        greet(device_at(0, dx))
    greet(device_at(1, 0))
    greet({"seq": 2 * z + 1 - y_hi, **device_at(1, 0)})
    greet(sibling)
    pl.semaphore_wait(barrier, n - 1 + X - 1 + 3)

    for slot in (4, 3, 1):
        w_copy(slot).start()
    for t in (0, 2, 1):
        each(1, lambda i: qkv_copy(t, i).start())
    ws_copy(0).start()
    for copy in local:
        copy.wait()
    for c in range(n):
        cut = slice(c * columns, (c + 1) * columns)
        go_t[cut, :] = go[:, cut].astype(F32).T.astype(BF16)

    def turn(src, dst, i):
        dst[:, block(i, rows)] = src[i].astype(F32).T.astype(BF16)

    def hand_on(slot, *nexts):
        w_copy(slot).wait_recv()
        for following in nexts:
            w_copy(following).start()
        ws_copy(slot).start()

    hand_on(4, 7, 5)
    each(1, lambda i: qkv_copy(0, i).wait_recv())

    k_rows = k_in.reshape(length, LANES)
    v_rows = v_in.reshape(length, LANES)

    def grad_attn(*slots):
        for slot in slots:
            ws_copy(slot).wait_recv()
        both = dot(jnp.concatenate([w_all[slot] for slot in slots], axis=0), go_t[...]).astype(BF16)
        for at, slot in enumerate(slots):
            i = behind(chip_at(slot // X, slot % X), s)
            g = both[at * LANES : (at + 1) * LANES]

            @pl.when(i == 0)
            def _():
                g_in[0] = g

            @pl.when(i > 0)
            def _():
                g_out[i] = g
                g_copy(i).start()

    def weight_part(b):
        first = b * batch
        each(max(first, 1), lambda i: o_copy(i).wait_recv(), first + batch)
        for i in range(batch):
            o_rows[i * half : (i + 1) * half, :] = o_in[first + i, my_half, :]
            o_rows[(batch + i) * half : (batch + i + 1) * half, :] = o_in[first + i, block(1 - core, half), :]
        for c in range(n):
            cut = slice(c * columns, (c + 1) * columns)
            part = dot(o_rows[...], go[:, cut]).astype(BF16)
            own_part[first : first + batch, :, cut] = part[: batch * half].reshape(batch, half, columns)
            sib_out[first : first + batch, :, cut] = part[batch * half :].reshape(batch, half, columns)
        sib_copy(b).start()

    def share(b):
        sib_copy(b).wait_recv()

        def send(i):
            dy, dx = where_to(i)
            pair = own_part[i].astype(F32) + sib_in[i].astype(F32)

            @pl.when(dx == 0)
            def _():
                home[dy] = pair

            @pl.when(dx > 0)
            def _():
                rs_out[i] = pair.astype(BF16)
                rs_copy(i).start()

        each(b * batch, send, (b + 1) * batch)

    def row_sum():
        for slot in range(1, 2 * X):
            if slot != X:
                rs_arrival(slot).wait_recv()
        for c in range(Z):
            cut = slice(c * quarter, (c + 1) * quarter)
            for dy in range(2):
                value = home[dy, :, cut]
                for dx in range(1, X):
                    value += rs_in[dy * X + dx, :, cut].astype(F32)
                total[c, dy] = value
                zs_out[c, dy] = value.astype(BF16)
        for k in range(1, Z):
            zs_copy(k).start()

    def patch_sum():
        for k in range(1, Z):
            zs_copy(k).wait_recv()
        for dy in range(2):
            value = total[z, dy]
            for k in range(1, Z):
                value += zs_in[k, dy].astype(F32)
            ys_out[dy] = value.astype(BF16)
        for k in range(3):
            ys_copy(k).start()
        ys_in[2 * y_hi + y] = ys_out[0]

    def weight_out():
        for k in range(3):
            ys_copy(k).wait_recv()
        value = ys_in[0].astype(F32)
        for at in range(1, 4):
            value += ys_in[at].astype(F32)
        done[...] = value.astype(BF16)
        for k in range(1, Z):
            gw_copy(k).start()
        gw_ref[:, block(z, quarter)] = done[...].astype(F32)

    def column(value):
        return jnp.broadcast_to(value, (8, wide)).T[:, 0:1]

    def scaled_rows(natural, scale):
        lane = lax.broadcasted_iota(jnp.int32, natural.shape, 1)
        first = jnp.where(lane < half, natural * scale[:rows], 0.0)
        second = jnp.where(lane < half, 0.0, natural * scale[rows:])
        return jnp.concatenate([first, second], axis=0).astype(BF16)

    def probs(i, with_out):
        @pl.when(i > 0)
        def _():
            qkv_copy(2, i).wait_recv()

        q = q_in[i].astype(F32)
        q_t[...] = split_heads(q.T).astype(BF16)

        def score_chunk(c, top):
            keys = block(c, CHUNK)
            value = dot(k_rows[keys, :], q_t[...])
            score[keys, :] = value
            return jnp.maximum(top, jnp.max(value.reshape(CHUNK // 8, 8, wide), axis=0))

        top = lax.fori_loop(0, chunks, score_chunk, jnp.full((8, wide), -jnp.inf, F32), unroll=True)
        top = jnp.max(top, axis=0, keepdims=True)
        if with_out:
            out_t[...] = jnp.zeros_like(out_t)

        def prob_chunk(c, norm):
            keys = block(c, CHUNK)
            p = jnp.exp2((score[keys, :] - top) * EXP_SCALE)
            low = p.astype(BF16)
            prob[keys, block(i, wide)] = low
            if with_out:
                out_t[...] += dot(v_t[:, keys], low)
            return norm + jnp.sum(p.reshape(CHUNK // 8, 8, wide), axis=0)

        norm = lax.fori_loop(0, chunks, prob_chunk, jnp.zeros((8, wide), F32), unroll=True)
        inverse = 1.0 / jnp.sum(norm, axis=0, keepdims=True)
        inv_sum[i] = jnp.broadcast_to(inverse, (8, wide))
        q_l[block(i, wide), :] = scaled_rows(q, column(inverse * SCALING))
        if with_out:
            send_out(i, out_t[...] * inverse)

    def send_out(i, wide_out):
        merged = merge_heads(wide_out)
        out_all[i] = merged

        @pl.when(i == 0)
        def _():
            o_in[0] = merged.astype(BF16)

        @pl.when(i > 0)
        def _():
            o_out[i] = merged.astype(BF16)
            o_copy(i).start()

    def early(i, carry):
        probs(i, False)

        @pl.when(i == 0)
        def _():
            hand_on(3, 2)
            hand_on(1)
            grad_attn(0, 4)

        @pl.when(i == 1)
        def _():
            hand_on(5, 6)
            grad_attn(3, 1)

        return carry

    def late(i, carry):
        probs(i, True)

        @pl.when(i == EARLY + 1)
        def _():
            hand_on(2)
            hand_on(6)

        @pl.when(i == EARLY + 2)
        def _():
            grad_attn(2, 6)

        @pl.when(i == batch + 2)
        def _():
            weight_part(0)

        @pl.when(i == batch + 3)
        def _():
            share(0)

        return carry

    lax.fori_loop(0, EARLY, early, 0)
    hand_on(7)
    turn(k_in, k_t, 0)
    each(1, lambda i: turn(k_in, k_t, i))
    grad_attn(5, 7)
    turn(v_in, v_t, 0)

    def arrive(i):
        qkv_copy(1, i).wait_recv()
        turn(v_in, v_t, i)

    each(1, arrive)
    each(0, lambda i: send_out(i, dot(v_t[...], prob[:, block(i, wide)]) * inv_sum[i, 0:1, :]), EARLY)
    lax.fori_loop(EARLY, n, late, 0)

    def prepare(i, carry):
        @pl.when(i > 0)
        def _():
            g_copy(i).wait_recv()

        g = g_in[i].astype(F32)
        g_t[:, block(i, wide)] = split_heads(g).astype(BF16)
        g_l[block(i, wide), :] = scaled_rows(g.T, column(inv_sum[i, 0:1, :]))
        product = out_all[i] * g
        both = jnp.concatenate(
            [
                jnp.sum(product[:half], axis=0, keepdims=True),
                jnp.sum(product[half:], axis=0, keepdims=True),
            ],
            axis=1,
        )
        row_dot[i] = jnp.broadcast_to(both, (8, wide))
        return carry

    lax.fori_loop(0, n, prepare, 0)
    weight_part(1)
    dq_t[...] = jnp.zeros_like(dq_t)
    share(1)

    def grad_q(i):
        return merge_heads(dq_t[:, block(i, wide)] * (inv_sum[i, 0:1, :] * SCALING)).T.astype(BF16)

    def backward(j, last):
        keys = block(j, span)

        def grad_chunk(i):
            cut = block(i, wide)
            grad_prob = dot(v_rows[keys, :], g_t[:, cut])
            grad_score = (prob[keys, cut].astype(F32) * (grad_prob - row_dot[i, 0:1, :])).astype(BF16)
            ds_buf[:, cut] = grad_score
            dq_t[:, cut] += dot(k_t[:, keys], grad_score)
            if last:
                dq_out[i] = grad_q(i)
                if i:
                    d_copy(0, i).start()

        for i in range(n):
            grad_chunk(i)
        grad_v = dot(prob[keys, :], g_l[...]).astype(BF16)
        grad_k = dot(ds_buf[...], q_l[...]).astype(BF16)

        for part in range(SPAN):
            i = j * SPAN + part
            cut = slice(part * rows, (part + 1) * rows)
            dk_out[i] = grad_k[cut]
            dv_out[i] = grad_v[cut]

            @pl.when(i > 0)
            def _():
                d_copy(1, i).start()
                d_copy(2, i).start()

    def backward_step(j, carry):
        backward(j, False)

        @pl.when(j == steps - 3)
        def _():
            row_sum()

        @pl.when(j == steps - 2)
        def _():
            patch_sum()

        return carry

    lax.fori_loop(0, steps - 1, backward_step, 0)
    backward(steps - 1, True)
    weight_out()
    for t in range(3):
        dqkv_ref[0, :, block(t * n + s, LANES)] = (dq_out, dk_out, dv_out)[t][0]

    def arrivals(i):
        for t in range(3):
            d_copy(t, i).wait_recv()

    each(1, arrivals)

    def sent(i):
        for t in range(3):
            qkv_copy(t, i).wait_send()
            d_copy(t, i).wait_send()
        g_copy(i).wait_send()
        o_copy(i).wait_send()

    each(1, sent)
    for slot in range(n):
        if slot:
            w_copy(slot).wait_send()
        ws_copy(slot).wait_send()
    sib_copy(0).wait_send()
    sib_copy(1).wait_send()
    for k in range(3):
        ys_copy(k).wait_send()
        zs_copy(k + 1).wait_send()
        gw_copy(k + 1).wait_send()
        gw_copy(k + 1).wait_recv()
        gw_ref[:, block(lax.rem(z + Z - k - 1, Z), quarter)] = gw_in[k + 1].astype(F32)

    def rs_sent(i):
        @pl.when(where_to(i)[1] > 0)
        def _():
            rs_copy(i).wait_send()

    each(0, rs_sent)


def on_device(n, queries, keys, values, out_proj, grad_out):
    rows, features = queries.shape[1:]
    share_rows, width = out_proj.shape
    length = n * rows
    wide = 2 * rows
    columns = width // n
    vmem = pltpu.VMEM
    dma = pltpu.SemaphoreType.DMA
    flat = vmem((n, rows, LANES), BF16)
    turned = vmem((n, LANES, rows), BF16)
    shares = vmem((n, HEAD_DIM, width), BF16)
    return pl.pallas_call(
        functools.partial(kernel, n, rows, width),
        out_shape=(
            vmem((1, rows, 3 * features), BF16),
            vmem((share_rows, width), F32),
        ),
        in_specs=[pl.BlockSpec(memory_space=pl.ANY)] * 5,
        out_specs=[pl.BlockSpec(memory_space=vmem)] * 2,
        scratch_shapes=[
            flat, flat, flat, turned,
            vmem((n, LANES, width), BF16),
            vmem((rows, width), BF16),
            vmem((width, rows), BF16),
            vmem((LANES, length), BF16),
            vmem((LANES, length), BF16),
            vmem((length, wide), F32),
            vmem((length, n * wide), BF16),
            vmem((LANES, wide), BF16),
            vmem((LANES, wide), F32),
            vmem((n, 8, wide), F32),
            vmem((n, LANES, rows), F32),
            vmem((n, 8, wide), F32),
            vmem((LANES, n * wide), BF16),
            vmem((n * wide, LANES), BF16),
            vmem((n * wide, LANES), BF16),
            vmem((SPAN * rows, n * wide), BF16),
            vmem((LANES, n * wide), F32),
            turned, turned, turned,
            vmem((n * HEAD_DIM, rows), BF16),
            shares, shares, shares, shares, shares,
            vmem((2, HEAD_DIM, width), F32),
            vmem((Z, 2, HEAD_DIM, width // Z), F32),
            vmem((Z, 2, HEAD_DIM, width // Z), BF16),
            vmem((Z, 2, HEAD_DIM, width // Z), BF16),
            vmem((2, HEAD_DIM, width // Z), BF16),
            vmem((4, HEAD_DIM, width // Z), BF16),
            vmem((HEAD_DIM, width // Z), BF16),
            vmem((Z, HEAD_DIM, width // Z), BF16),
            flat, flat, flat,
            dma((3, n)), dma((3, n)),
            dma((n,)), dma((n,)), dma((n,)), dma((n,)),
            dma((n,)), dma((n,)), dma((n,)), dma((n,)),
            dma((2,)), dma((2,)), dma((n,)), dma((n,)),
            dma((Z,)), dma((Z,)), dma((3,)), dma((3,)), dma((Z,)), dma((Z,)),
            dma((3, n)), dma((3, n)), dma((5,)),
        ],
        compiler_params=pltpu.CompilerParams(
            collective_id=0, has_side_effects=True, vmem_limit_bytes=60 << 20
        ),
    )(queries, keys, values, out_proj, grad_out)


def solution(mesh):
    return jax.shard_map(
        functools.partial(on_device, mesh.shape["seq"]),
        mesh=mesh,
        in_specs=(
            P("dp", "seq", None),
            P("dp", "seq", None),
            P("dp", "seq", None),
            P("dp", None),
            P("dp", "seq", None),
        ),
        out_specs=(P("dp", "seq", None), P("dp", None)),
        check_vma=False,
    )
```
